512 devices in a mesh: kv: 8 (over x, core), seq: 64 (over z, y).
Axes of the slice: x: 4, y: 8, z: 8, core: 2. Of those that a mesh axis runs over, the one named last changes fastest.
Arguments:
- queries: bfloat16 [512, 4096], P(('kv', 'seq')), may hold values from -6 to 6
- out_grad: bfloat16 [512, 4096], P(('kv', 'seq')), may hold values from -3072 to 3072
- saved_out: bfloat16 [512, 4096], P(('kv', 'seq')), may hold values from -1.5 to 1.5
- saved_lse: float32 [512, 32], P(('kv', 'seq')), as said below
- video_keys: bfloat16 [16384, 1024], P('seq', 'kv'), may hold values from -6 to 6
- video_values: bfloat16 [16384, 1024], P('seq', 'kv'), may hold values from -6 to 6
Outputs:
- grad_queries: bfloat16 [512, 4096], P(('kv', 'seq'))
- grad_keys: bfloat16 [16384, 1024], P('seq', 'kv')
- grad_values: bfloat16 [16384, 1024], P('seq', 'kv')
The draws below stay inside these ranges and needn't reach their ends.
Inputs may be any that keep to these rules, and one draw needn't show every extreme that they name: saved_lse lies between log(16384) and log(16384) + 1.5.
All inputs are finite; a program needn't handle non-finite values.
Results may differ from the reference program's by a relative error of at most 0.0057.
Values may be sent and summed in bfloat16 or wider, within the bound.
A program may use at most 64 MiB of HBM per device.

```python
import math
import jax
import jax.numpy as jnp

HD = 128
GROUP = 4
QUERIES = 512
KV_HEADS = 8
HEADS = 32
KEYS = 16384


def draw_saved_lse(key, part):
    log_keys = jnp.log(jnp.float32(KEYS))
    offsets = jax.random.uniform(key, (QUERIES, HEADS), jnp.float32, 0.3, 1.2)
    return log_keys + offsets


def steps_of(stream_key, shape, cuts, least, largest):
    loudness = 1.0
    for axis_at, shards_of in cuts:
        heights = jax.random.uniform(jax.random.fold_in(jax.random.fold_in(stream_key, 6), axis_at), (shards_of,), jnp.float32, least / len(cuts), largest / len(cuts))
        loudness = loudness * jnp.repeat(jnp.exp(heights), shape[axis_at] // shards_of).reshape((-1,) + (1,) * (len(shape) - 1 - axis_at))
    return loudness


def noise(rng, shape, width, limit, cuts=(), kind=jnp.bfloat16):
    result = width * jax.random.normal(rng, shape, jnp.float32)
    if cuts:
        result = result * steps_of(rng, shape, cuts, -0.22, 0.18)
    return jnp.clip(result, -limit, limit).astype(kind)


def setup_inputs(seed: int = 0) -> dict:
    key_list = jax.random.split(jax.random.key(seed), 7)
    return {
        "queries": noise(key_list[0], (QUERIES, HEADS * HD), 1.0, 6.0, ((0, 512),)),
        "out_grad": noise(key_list[1], (QUERIES, HEADS * HD), (KEYS // 32), 3072.0, ((0, 512),)),
        "saved_out": noise(key_list[2], (QUERIES, HEADS * HD), 0.25, 1.5, ((0, 512),)),
        "saved_lse": draw_saved_lse(jax.random.fold_in(key_list[6], 71), 0),
        "video_keys": noise(key_list[4], (KEYS, KV_HEADS * HD), 1.0, 6.0, ((0, 64), (1, 8))),
        "video_values": noise(key_list[5], (KEYS, KV_HEADS * HD), 1.0, 6.0, ((0, 64), (1, 8))),
    }


def reference(queries, out_grad, saved_out, saved_lse, video_keys, video_values):
    score_scale = 1.0 / math.sqrt(HD)
    products = out_grad.astype(jnp.float32) * saved_out.astype(jnp.float32)
    row_delta = products.reshape(QUERIES, HEADS, HD).sum(axis=2)
    query_columns = []
    key_columns = []
    value_columns = []
    for kv_index in range(KV_HEADS):
        key_block = video_keys[:, kv_index * HD:(kv_index + 1) * HD]
        value_block = video_values[:, kv_index * HD:(kv_index + 1) * HD]
        key_total = jnp.zeros((KEYS, HD), jnp.float32)
        value_total = jnp.zeros((KEYS, HD), jnp.float32)
        for member in range(GROUP):
            head_index = kv_index * GROUP + member
            query_head = queries[:, head_index * HD:(head_index + 1) * HD]
            grad_head = out_grad[:, head_index * HD:(head_index + 1) * HD]
            scores = jnp.dot(query_head, key_block.T, preferred_element_type=jnp.float32) * score_scale
            probs = jnp.exp(scores - saved_lse[:, head_index:head_index + 1])
            probs_half = probs.astype(jnp.bfloat16)
            value_total = value_total + jnp.dot(probs_half.T, grad_head, preferred_element_type=jnp.float32)
            dprobs = jnp.dot(grad_head, value_block.T, preferred_element_type=jnp.float32)
            dscores = (probs * (dprobs - row_delta[:, head_index:head_index + 1])).astype(jnp.bfloat16)
            key_total = key_total + jnp.dot(dscores.T, query_head, preferred_element_type=jnp.float32)
            query_columns.append((jnp.dot(dscores, key_block, preferred_element_type=jnp.float32) * score_scale).astype(jnp.bfloat16))
        key_columns.append((key_total * score_scale).astype(jnp.bfloat16))
        value_columns.append(value_total.astype(jnp.bfloat16))
    return (jnp.concatenate(query_columns, axis=1), jnp.concatenate(key_columns, axis=1), jnp.concatenate(value_columns, axis=1))
```

```python
import functools
import math

import jax
import jax.numpy as jnp
from jax import lax
from jax.experimental import pallas as pl
from jax.experimental.pallas import tpu as pltpu
from jax.sharding import PartitionSpec as P

MESH = pl.DeviceIdType.MESH
LANES = 128


def other_coords(count):
    return sorted(range(1, count), key=lambda d: (min(d, count - d), d))


def kernel(
    sizes,
    q_ref,
    grad_ref,
    out_ref,
    lse_ref,
    keys_ref,
    values_ref,
    dq_ref,
    dkeys_ref,
    dvalues_ref,
    packet,
    packet_aux,
    got,
    got_aux,
    held0,
    held1,
    block0,
    block1,
    aux0,
    aux1,
    terms0,
    terms1,
    away0,
    away1,
    come0,
    come1,
    turned0,
    turned1,
    dq_away0,
    dq_away1,
    dq_come0,
    dq_come1,
    back,
    back_come,
    load_sem,
    exchange_send,
    exchange_recv,
    ring_send,
    ring_recv,
    block_send,
    block_recv,
    sum_send,
    sum_recv,
    dq_send,
    dq_recv,
    back_send,
    back_recv,
):
    groups, ny, nz, heads, width, half_keys = sizes
    counts = (ny, nz)
    held, block, aux = (held0, held1), (block0, block1), (aux0, aux1)
    terms, away, come = (terms0, terms1), (away0, away1), (come0, come1)
    turned = (turned0, turned1)
    dq_away, dq_come = (dq_away0, dq_away1), (dq_come0, dq_come1)
    pairs = groups * heads
    scale = 1.0 / math.sqrt(width)

    mine = lax.axis_index("kv")
    place = lax.axis_index("seq")
    y, z = lax.rem(place, ny), lax.div(place, ny)
    position = (y, z)

    def peer(axis, index):
        return (mine, z * ny + index) if axis == 0 else (mine, index * ny + y)

    def around(axis, step):
        return lax.rem(position[axis] + (step % counts[axis]), counts[axis])

    def remote(src, dst, send, recv, device):
        return pltpu.make_async_remote_copy(
            src_ref=src, dst_ref=dst, send_sem=send, recv_sem=recv, device_id=device, device_id_type=MESH
        )

    barrier = pltpu.get_barrier_semaphore()
    for d in range(1, groups):
        pl.semaphore_signal(barrier, inc=1, device_id=(lax.rem(mine + d, groups), place), device_id_type=MESH)
    for axis in (0, 1):
        for d in range(1, counts[axis]):
            pl.semaphore_signal(barrier, inc=1, device_id=peer(axis, around(axis, d)), device_id_type=MESH)

    loads = []
    for half in (0, 1):
        for part, source in ((0, keys_ref), (1, values_ref)):
            copy = pltpu.make_async_copy(
                source.at[pl.ds(half * half_keys, half_keys), :],
                held[half].at[position[half], part],
                load_sem.at[half, part],
            )
            copy.start()
            loads.append(copy)

    def rows_of(ref):
        flat = ref[...].astype(jnp.float32)
        return jnp.concatenate([flat[:, i * width : (i + 1) * width] for i in range(pairs)], axis=0)

    q_rows, grad_rows, out_rows = rows_of(q_ref), rows_of(grad_ref), rows_of(out_ref)
    delta_column = jnp.sum(grad_rows * out_rows, axis=1, keepdims=True)
    eye = lax.broadcasted_iota(jnp.int32, (pairs, pairs), 0) == lax.broadcasted_iota(jnp.int32, (pairs, pairs), 1)
    lse_column = jnp.sum(
        jnp.where(eye, jnp.broadcast_to(lse_ref[...], (pairs, pairs)), 0.0), axis=1, keepdims=True
    )
    lane = lax.broadcasted_iota(jnp.int32, (pairs, LANES), 1)
    member = lax.rem(lax.broadcasted_iota(jnp.int32, (pairs, LANES), 0), heads)
    spot = lane == mine * heads + member
    lse_spots = jnp.where(spot, jnp.broadcast_to(lse_column, (pairs, LANES)), 0.0)
    delta_spots = jnp.where(spot, jnp.broadcast_to(delta_column, (pairs, LANES)), 0.0)
    for group in range(groups):
        rows = slice(group * heads, (group + 1) * heads)
        packet[group] = jnp.concatenate([q_rows[rows], grad_rows[rows]], axis=0).astype(jnp.bfloat16)
        packet_aux[group] = jnp.concatenate([lse_spots[rows], delta_spots[rows]], axis=0)

    pl.semaphore_wait(barrier, groups - 1 + ny - 1 + nz - 1)

    def exchange(target, origin):
        device = (target, place)
        return (
            remote(packet.at[target], got.at[origin], exchange_send.at[target, 0], exchange_recv.at[origin, 0], device),
            remote(
                packet_aux.at[target],
                got_aux.at[origin],
                exchange_send.at[target, 1],
                exchange_recv.at[origin, 1],
                device,
            ),
        )

    for d in other_coords(groups):
        for copy in exchange(lax.rem(mine + d, groups), mine):
            copy.start()
    got[mine] = packet[mine]
    got_aux[mine] = packet_aux[mine]

    def ring_parts(axis, direction, step):
        return (0, 1) if step < counts[axis] // 2 - 1 else (direction,)

    def ring_copy(axis, direction, step, part, arriving=False):
        reach = step + 1 if arriving else step
        origin = around(axis, -reach if direction == 0 else reach)
        ref = held[axis].at[origin, part]
        return remote(
            ref,
            ref,
            ring_send.at[axis, direction, step, part],
            ring_recv.at[axis, direction, step, part],
            peer(axis, around(axis, 1 if direction == 0 else -1)),
        )

    def ring_step(step):
        for part in (0, 1):
            for axis in (0, 1):
                if step >= counts[axis] // 2:
                    continue
                for direction in (0, 1):
                    if part in ring_parts(axis, direction, step):
                        if step:
                            ring_copy(axis, direction, step - 1, part, True).wait_recv()
                        ring_copy(axis, direction, step, part).start()

    for copy in loads:
        copy.wait()
    ring_step(0)

    for d in range(1, groups):
        for copy in exchange(mine, lax.rem(mine + d, groups)):
            copy.wait_recv()
    got_rows = got[...].astype(jnp.float32)
    own_block = jnp.concatenate(
        [got_rows[i, :heads] for i in range(groups)] + [got_rows[i, heads:] for i in range(groups)], axis=0
    ).astype(jnp.bfloat16)
    got_sum = jnp.sum(got_aux[...], axis=0)
    own_aux = [
        jnp.sum(got_sum[:heads], axis=0, keepdims=True),
        jnp.sum(got_sum[heads:], axis=0, keepdims=True),
    ]
    per_row = LANES // pairs
    lane_row = lax.broadcasted_iota(jnp.int32, (1, LANES), 1)

    def block_copies(half, target, origin):
        axis = 1 - half
        device = peer(axis, target)
        return (
            remote(
                block[half].at[origin],
                block[half].at[origin],
                block_send.at[half, target, 0],
                block_recv.at[half, origin, 0],
                device,
            ),
            remote(
                aux[half].at[origin],
                aux[half].at[origin],
                block_send.at[half, target, 1],
                block_recv.at[half, origin, 1],
                device,
            ),
        )

    for half in (0, 1):
        at = position[1 - half]
        block[half][at] = own_block
        inside = lax.div(lane_row, pairs) == lax.rem(at, per_row)
        spread = []
        for vector in own_aux:
            total = vector
            for k in range(1, per_row):
                total = total + pltpu.roll(vector, k * pairs, 1)
            spread.append(jnp.where(inside, total, 0.0))
        aux[half][at] = jnp.concatenate(spread, axis=0)
    for half in (0, 1):
        axis = 1 - half
        for d in reversed(other_coords(counts[axis])):
            for copy in block_copies(half, around(axis, d), position[axis]):
                copy.start()

    most = max(counts) // 2
    for step in range(1, most):
        ring_step(step)

    lse_rows, delta_rows = [], []
    for half in (0, 1):
        axis = 1 - half
        for d in other_coords(counts[axis]):
            for copy in block_copies(half, position[axis], around(axis, d)):
                copy.wait_recv()
        total_pairs = counts[axis] * pairs
        for index, found in ((0, lse_rows), (1, delta_rows)):
            pieces = []
            for first in range(0, counts[axis], per_row):
                piece = aux[half][first, index : index + 1, :]
                for j in range(first + 1, min(first + per_row, counts[axis])):
                    piece = piece + aux[half][j, index : index + 1, :]
                pieces.append(piece)
            found.append(jnp.concatenate(pieces, axis=1)[:, :total_pairs])
        turned[half][...] = jnp.zeros_like(turned[half])

    def chunk(half, index):
        total_pairs = counts[1 - half] * pairs
        q_all = block[half][:, :pairs, :].reshape(total_pairs, width)
        grad_all = block[half][:, pairs:, :].reshape(total_pairs, width)
        key, value = held[half][index, 0], held[half][index, 1]
        across = (((1,), (1,)), ((), ()))
        scores = lax.dot_general(key, q_all, across, preferred_element_type=jnp.float32)
        probs = jnp.exp(scores * scale - lse_rows[half])
        dprobs = lax.dot_general(value, grad_all, across, preferred_element_type=jnp.float32)
        dscores = (probs * (dprobs - delta_rows[half])).astype(jnp.bfloat16)
        dvalue = jnp.dot(probs.astype(jnp.bfloat16), grad_all, preferred_element_type=jnp.float32)
        dkey = jnp.dot(dscores, q_all, preferred_element_type=jnp.float32)
        turned[half][...] += lax.dot_general(
            key, dscores, (((0,), (0,)), ((), ())), preferred_element_type=jnp.float32
        )
        return dkey * scale, dvalue

    def sum_copy(axis, direction, step, part):
        return remote(
            away[axis].at[direction, step, part],
            come[axis].at[direction, step, part],
            sum_send.at[axis, direction, step, part],
            sum_recv.at[axis, direction, step, part],
            peer(axis, around(axis, 1 if direction == 0 else -1)),
        )

    def ring_target(axis, direction, step):
        reach = counts[axis] // 2 - step
        return reach if direction == 0 else counts[axis] - reach

    for half in (0, 1):
        reach = counts[half] // 2
        for direction in (0, 1):
            ring_copy(half, direction, reach - 1, direction, True).wait_recv()
        found = chunk(half, around(half, reach))
        for direction in (0, 1):
            away[half][direction, 0, direction] = found[direction].astype(jnp.bfloat16)
            sum_copy(half, direction, 0, direction).start()

    for half in (0, 1):
        reach = counts[half] // 2
        if reach > 1:
            for direction in (0, 1):
                ring_copy(half, direction, reach - 2, 1 - direction, True).wait_recv()
    for step in range(1, most):
        for half in (0, 1):
            if step < counts[half] // 2:
                for direction in (0, 1):
                    offset = ring_target(half, direction, step)
                    found = chunk(half, around(half, offset))
                    terms[half][offset, 0] = found[0]
                    terms[half][offset, 1] = found[1]
    for half in (0, 1):
        found = chunk(half, position[half])
        terms[half][0, 0] = found[0]
        terms[half][0, 1] = found[1]

    def dq_copy(half, target, origin):
        return remote(
            dq_away[half].at[target],
            dq_come[half].at[origin],
            dq_send.at[half, target],
            dq_recv.at[half, origin],
            peer(1 - half, target),
        )

    for half in (0, 1):
        axis = 1 - half
        dq_away[half][...] = jnp.transpose(turned[half][...]).reshape(counts[axis], pairs, width)
        for d in reversed(other_coords(counts[axis])):
            dq_copy(half, around(axis, d), position[axis]).start()

    def has_upstream(direction, step, part):
        return step > 1 or (step == 1 and part == direction)

    for step in range(1, most):
        for part in (0, 1):
            for half in (0, 1):
                if step >= counts[half] // 2:
                    continue
                for direction in (0, 1):
                    total = terms[half][ring_target(half, direction, step), part]
                    if has_upstream(direction, step, part):
                        sum_copy(half, direction, step - 1, part).wait_recv()
                        total = total + come[half][direction, step - 1, part].astype(jnp.float32)
                    away[half][direction, step, part] = total.astype(jnp.bfloat16)
                    sum_copy(half, direction, step, part).start()

    dq_sum = dq_away[0][position[1]] + dq_away[1][position[0]]
    for half in (0, 1):
        axis = 1 - half
        for d in other_coords(counts[axis]):
            j = around(axis, d)
            dq_copy(half, position[axis], j).wait_recv()
            dq_sum = dq_sum + dq_come[half][j]
    dq_rows = dq_sum * scale
    for group in range(groups):
        back[group] = dq_rows[group * heads : (group + 1) * heads].astype(jnp.bfloat16)

    def back_copy(target, origin):
        return remote(
            back.at[target], back_come.at[origin], back_send.at[target], back_recv.at[origin], (target, place)
        )

    for d in other_coords(groups):
        back_copy(lax.rem(mine + d, groups), mine).start()
    back_come[mine] = back[mine]

    for half in (0, 1):
        last = counts[half] // 2 - 1
        rows = pl.ds(half * half_keys, half_keys)
        for part, result in ((0, dkeys_ref), (1, dvalues_ref)):
            total = terms[half][0, part]
            for direction in (0, 1):
                if last > 0 or part == direction:
                    sum_copy(half, direction, last, part).wait_recv()
                    total = total + come[half][direction, last, part].astype(jnp.float32)
            result[rows, :] = total.astype(jnp.bfloat16)

    for d in range(1, groups):
        back_copy(mine, lax.rem(mine + d, groups)).wait_recv()
    dq_ref[...] = back_come[...]

    for d in range(1, groups):
        target = lax.rem(mine + d, groups)
        for copy in exchange(target, mine):
            copy.wait_send()
        back_copy(target, mine).wait_send()
    for half in (0, 1):
        axis = 1 - half
        for d in range(1, counts[axis]):
            target = around(axis, d)
            for copy in block_copies(half, target, position[axis]):
                copy.wait_send()
            dq_copy(half, target, position[axis]).wait_send()
        for direction in (0, 1):
            for step in range(counts[half] // 2):
                for part in ring_parts(half, direction, step):
                    ring_copy(half, direction, step, part).wait_send()
                for part in (0, 1) if step else (direction,):
                    sum_copy(half, direction, step, part).wait_send()


def shards(ny, nz, queries, out_grad, saved_out, saved_lse, video_keys, video_values):
    groups = lax.axis_size("kv")
    width = video_keys.shape[1]
    heads = queries.shape[1] // (groups * width)
    key_rows = video_keys.shape[0]
    half_keys = key_rows // 2
    pairs = groups * heads
    counts = (ny, nz)
    bf16, f32 = jnp.bfloat16, jnp.float32
    dma = pltpu.SemaphoreType.DMA
    most = max(counts)
    across = (counts[1], counts[0])
    scratch = (
        [
            pltpu.VMEM((groups, 2 * heads, width), bf16),
            pltpu.VMEM((groups, 2 * heads, LANES), f32),
            pltpu.VMEM((groups, 2 * heads, width), bf16),
            pltpu.VMEM((groups, 2 * heads, LANES), f32),
        ]
        + [pltpu.VMEM((n, 2, half_keys, width), bf16) for n in counts]
        + [pltpu.VMEM((n, 2 * pairs, width), bf16) for n in across]
        + [pltpu.VMEM((n, 2, LANES), f32) for n in across]
        + [pltpu.VMEM((n, 2, half_keys, width), f32) for n in counts]
        + [pltpu.VMEM((2, n // 2, 2, half_keys, width), bf16) for n in counts]
        + [pltpu.VMEM((2, n // 2, 2, half_keys, width), bf16) for n in counts]
        + [pltpu.VMEM((width, n * pairs), f32) for n in across]
        + [pltpu.VMEM((n, pairs, width), f32) for n in across]
        + [pltpu.VMEM((n, pairs, width), f32) for n in across]
        + [pltpu.VMEM((groups, heads, width), bf16), pltpu.VMEM((groups, heads, width), bf16)]
        + [
            dma((2, 2)),
            dma((groups, 2)),
            dma((groups, 2)),
            dma((2, 2, most // 2, 2)),
            dma((2, 2, most // 2, 2)),
            dma((2, most, 2)),
            dma((2, most, 2)),
            dma((2, 2, most // 2, 2)),
            dma((2, 2, most // 2, 2)),
            dma((2, most)),
            dma((2, most)),
            dma((groups,)),
            dma((groups,)),
        ]
    )
    vmem = pl.BlockSpec(memory_space=pltpu.VMEM)
    dq, dkeys, dvalues = pl.pallas_call(
        functools.partial(kernel, (groups, ny, nz, heads, width, half_keys)),
        out_shape=(
            jax.ShapeDtypeStruct((groups, heads, width), bf16),
            jax.ShapeDtypeStruct((key_rows, width), bf16),
            jax.ShapeDtypeStruct((key_rows, width), bf16),
        ),
        in_specs=[vmem] * 4 + [pl.BlockSpec(memory_space=pl.ANY)] * 2,
        out_specs=(vmem, vmem, vmem),
        scratch_shapes=scratch,
        compiler_params=pltpu.CompilerParams(
            collective_id=0, has_side_effects=True, vmem_limit_bytes=40 * 1024 * 1024
        ),
        name="attention_backward",
    )(queries, out_grad, saved_out, saved_lse, video_keys, video_values)
    return dq.reshape(1, groups * heads * width), dkeys, dvalues


def solution(mesh):
    seq = mesh.shape["seq"]
    ny = 1
    while ny * ny < seq:
        ny *= 2
    nz = seq // ny
    rows = P(("kv", "seq"), None)
    keys = P("seq", "kv")
    return jax.shard_map(
        functools.partial(shards, ny, nz),
        mesh=mesh,
        in_specs=(rows, rows, rows, rows, keys, keys),
        out_specs=(rows, keys, keys),
        check_vma=False,
    )
```

```python
import functools
import math

import jax
import jax.numpy as jnp
from jax import lax
from jax.experimental import pallas as pl
from jax.experimental.pallas import tpu as pltpu
from jax.sharding import PartitionSpec as P

MESH = pl.DeviceIdType.MESH
LANES = 128


def other_coords(count):
    return sorted(range(1, count), key=lambda d: (min(d, count - d), d))


def kernel(
    sizes,
    q_hbm,
    grad_hbm,
    out_hbm,
    lse_hbm,
    keys_ref,
    values_ref,
    dq_ref,
    dkeys_ref,
    dvalues_ref,
    q_ref,
    grad_ref,
    out_ref,
    lse_ref,
    packet,
    packet_aux,
    got,
    got_aux,
    held0,
    held1,
    block0,
    block1,
    aux0,
    aux1,
    terms0,
    terms1,
    away0,
    away1,
    come0,
    come1,
    turned0,
    turned1,
    dq_full0,
    dq_full1,
    dq_away0,
    dq_away1,
    dq_come0,
    dq_come1,
    back,
    back_come,
    row_sem,
    load_sem,
    exchange_send,
    exchange_recv,
    ring_send,
    ring_recv,
    block_send,
    block_recv,
    sum_send,
    sum_recv,
    dq_send,
    dq_recv,
    back_send,
    back_recv,
):
    groups, ny, nz, heads, width, half_keys, pieces = sizes
    piece_rows = half_keys // pieces
    counts = (ny, nz)
    held, block, aux = (held0, held1), (block0, block1), (aux0, aux1)
    terms, away, come = (terms0, terms1), (away0, away1), (come0, come1)
    turned = (turned0, turned1)
    dq_full = (dq_full0, dq_full1)
    dq_away, dq_come = (dq_away0, dq_away1), (dq_come0, dq_come1)
    pairs = groups * heads
    scale = 1.0 / math.sqrt(width)

    mine = lax.axis_index("kv")
    place = lax.axis_index("seq")
    y, z = lax.rem(place, ny), lax.div(place, ny)
    position = (y, z)

    def peer(axis, index):
        return (mine, z * ny + index) if axis == 0 else (mine, index * ny + y)

    def around(axis, step):
        return lax.rem(position[axis] + (step % counts[axis]), counts[axis])

    def remote(src, dst, send, recv, device):
        return pltpu.make_async_remote_copy(
            src_ref=src, dst_ref=dst, send_sem=send, recv_sem=recv, device_id=device, device_id_type=MESH
        )

    row_loads = []
    for index, (source, target) in enumerate(
        ((q_hbm, q_ref), (grad_hbm, grad_ref), (out_hbm, out_ref), (lse_hbm, lse_ref))
    ):
        copy = pltpu.make_async_copy(source, target, row_sem.at[index])
        copy.start()
        row_loads.append(copy)

    barrier = pltpu.get_barrier_semaphore()
    for d in range(1, groups):
        pl.semaphore_signal(barrier, inc=1, device_id=(lax.rem(mine + d, groups), place), device_id_type=MESH)
    for axis in (0, 1):
        for d in range(1, counts[axis]):
            pl.semaphore_signal(barrier, inc=1, device_id=peer(axis, around(axis, d)), device_id_type=MESH)

    loads = []
    for half in (0, 1):
        for part, source in ((0, keys_ref), (1, values_ref)):
            copy = pltpu.make_async_copy(
                source.at[pl.ds(half * half_keys, half_keys), :],
                held[half].at[position[half], part],
                load_sem.at[half, part],
            )
            copy.start()
            loads.append(copy)

    for copy in row_loads:
        copy.wait()

    def rows_of(ref):
        flat = ref[...].astype(jnp.float32)
        return jnp.concatenate([flat[:, i * width : (i + 1) * width] for i in range(pairs)], axis=0)

    q_rows, grad_rows, out_rows = rows_of(q_ref), rows_of(grad_ref), rows_of(out_ref)
    delta_column = jnp.sum(grad_rows * out_rows, axis=1, keepdims=True)
    eye = lax.broadcasted_iota(jnp.int32, (pairs, pairs), 0) == lax.broadcasted_iota(jnp.int32, (pairs, pairs), 1)
    lse_column = jnp.sum(
        jnp.where(eye, jnp.broadcast_to(lse_ref[...], (pairs, pairs)), 0.0), axis=1, keepdims=True
    )
    lane = lax.broadcasted_iota(jnp.int32, (pairs, LANES), 1)
    member = lax.rem(lax.broadcasted_iota(jnp.int32, (pairs, LANES), 0), heads)
    spot = lane == mine * heads + member
    lse_spots = jnp.where(spot, jnp.broadcast_to(lse_column, (pairs, LANES)), 0.0)
    delta_spots = jnp.where(spot, jnp.broadcast_to(delta_column, (pairs, LANES)), 0.0)
    for group in range(groups):
        rows = slice(group * heads, (group + 1) * heads)
        packet[group] = jnp.concatenate([q_rows[rows], grad_rows[rows]], axis=0).astype(jnp.bfloat16)
        packet_aux[group] = jnp.concatenate([lse_spots[rows], delta_spots[rows]], axis=0)

    pl.semaphore_wait(barrier, groups - 1 + ny - 1 + nz - 1)

    def exchange(target, origin):
        device = (target, place)
        return (
            remote(packet.at[target], got.at[origin], exchange_send.at[0], exchange_recv.at[origin, 0], device),
            remote(
                packet_aux.at[target],
                got_aux.at[origin],
                exchange_send.at[0],
                exchange_recv.at[origin, 1],
                device,
            ),
        )

    for d in other_coords(groups):
        for copy in exchange(lax.rem(mine + d, groups), mine):
            copy.start()
    got[mine] = packet[mine]
    got_aux[mine] = packet_aux[mine]

    def ring_parts(axis, direction, step):
        kinds = (0, 1) if step < counts[axis] // 2 - 1 else (direction,)
        return [(kind, piece) for kind in kinds for piece in range(pieces)]

    every_part = [(kind, piece) for kind in (0, 1) for piece in range(pieces)]

    def ring_copy(axis, direction, step, part, arriving=False):
        reach = step + 1 if arriving else step
        origin = around(axis, -reach if direction == 0 else reach)
        kind, piece = part
        ref = held[axis].at[origin, kind, pl.ds(piece * piece_rows, piece_rows), :]
        slot = kind * pieces + piece
        return remote(
            ref,
            ref,
            ring_send.at[0],
            ring_recv.at[axis, direction, step, slot],
            peer(axis, around(axis, 1 if direction == 0 else -1)),
        )

    def ring_step(step):
        for part in every_part:
            for axis in (0, 1):
                if step >= counts[axis] // 2:
                    continue
                for direction in (0, 1):
                    if part in ring_parts(axis, direction, step):
                        if step:
                            ring_copy(axis, direction, step - 1, part, True).wait_recv()
                        ring_copy(axis, direction, step, part).start()

    most = max(counts) // 2
    for copy in loads:
        copy.wait()
    for step in range(min(2, most)):
        ring_step(step)

    for d in range(1, groups):
        for copy in exchange(mine, lax.rem(mine + d, groups)):
            copy.wait_recv()
    got_rows = got[...].astype(jnp.float32)
    own_block = jnp.concatenate(
        [got_rows[i, :heads] for i in range(groups)] + [got_rows[i, heads:] for i in range(groups)], axis=0
    ).astype(jnp.bfloat16)
    got_sum = jnp.sum(got_aux[...], axis=0)
    own_aux = [
        jnp.sum(got_sum[:heads], axis=0, keepdims=True),
        jnp.sum(got_sum[heads:], axis=0, keepdims=True),
    ]
    per_row = LANES // pairs
    lane_row = lax.broadcasted_iota(jnp.int32, (1, LANES), 1)

    def block_copies(half, target, origin):
        axis = 1 - half
        device = peer(axis, target)
        return (
            remote(
                block[half].at[origin],
                block[half].at[origin],
                block_send.at[0],
                block_recv.at[half, origin, 0],
                device,
            ),
            remote(
                aux[half].at[origin],
                aux[half].at[origin],
                block_send.at[0],
                block_recv.at[half, origin, 1],
                device,
            ),
        )

    for half in (0, 1):
        at = position[1 - half]
        block[half][at] = own_block
        inside = lax.div(lane_row, pairs) == lax.rem(at, per_row)
        spread = []
        for vector in own_aux:
            total = vector
            for k in range(1, per_row):
                total = total + pltpu.roll(vector, k * pairs, 1)
            spread.append(jnp.where(inside, total, 0.0))
        aux[half][at] = jnp.concatenate(spread, axis=0)
    for half in (0, 1):
        axis = 1 - half
        for d in reversed(other_coords(counts[axis])):
            for copy in block_copies(half, around(axis, d), position[axis]):
                copy.start()

    for step in range(2, most - 1):
        ring_step(step)

    lse_rows, delta_rows = [], []
    for half in (0, 1):
        axis = 1 - half
        for d in other_coords(counts[axis]):
            for copy in block_copies(half, position[axis], around(axis, d)):
                copy.wait_recv()
        total_pairs = counts[axis] * pairs
        for index, found in ((0, lse_rows), (1, delta_rows)):
            sums = []
            for first in range(0, counts[axis], per_row):
                piece = aux[half][first, index : index + 1, :]
                for j in range(first + 1, min(first + per_row, counts[axis])):
                    piece = piece + aux[half][j, index : index + 1, :]
                sums.append(piece)
            found.append(jnp.concatenate(sums, axis=1)[:, :total_pairs])
        turned[half][...] = jnp.zeros_like(turned[half])

    def chunk(half, offsets):
        total_pairs = counts[1 - half] * pairs
        q_all = block[half][:, :pairs, :].reshape(total_pairs, width)
        grad_all = block[half][:, pairs:, :].reshape(total_pairs, width)
        places = [around(half, offset) for offset in offsets]
        key = jnp.concatenate([held[half][at, 0] for at in places], axis=0)
        value = jnp.concatenate([held[half][at, 1] for at in places], axis=0)
        across = (((1,), (1,)), ((), ()))
        scores = lax.dot_general(key, q_all, across, preferred_element_type=jnp.float32)
        probs = jnp.exp(scores * scale - lse_rows[half])
        dprobs = lax.dot_general(value, grad_all, across, preferred_element_type=jnp.float32)
        dscores = (probs * (dprobs - delta_rows[half])).astype(jnp.bfloat16)
        dvalue = jnp.dot(probs.astype(jnp.bfloat16), grad_all, preferred_element_type=jnp.float32)
        dkey = jnp.dot(dscores, q_all, preferred_element_type=jnp.float32) * scale
        turned[half][...] += lax.dot_general(
            key, dscores, (((0,), (0,)), ((), ())), preferred_element_type=jnp.float32
        )
        for index, offset in enumerate(offsets):
            rows = slice(index * half_keys, (index + 1) * half_keys)
            terms[half][offset % counts[half], 0] = dkey[rows]
            terms[half][offset % counts[half], 1] = dvalue[rows]

    def sum_parts(direction, step):
        return every_part if step else [(direction, piece) for piece in range(pieces)]

    def sum_copy(axis, direction, step, part):
        kind, piece = part
        rows = pl.ds(piece * piece_rows, piece_rows)
        slot = kind * pieces + piece
        return remote(
            away[axis].at[direction, step, kind, rows, :],
            come[axis].at[direction, step, kind, rows, :],
            sum_send.at[0],
            sum_recv.at[axis, direction, step, slot],
            peer(axis, around(axis, 1 if direction == 0 else -1)),
        )

    def sum_step(step, fresh):
        for part in every_part:
            kind, piece = part
            rows = pl.ds(piece * piece_rows, piece_rows)
            for half in (0, 1):
                reach = counts[half] // 2 - step
                for direction in (0, 1):
                    if reach < 1 or part not in sum_parts(direction, step):
                        continue
                    if fresh != (step == 0 or part not in sum_parts(direction, step - 1)):
                        continue
                    offset = reach if direction == 0 else counts[half] - reach
                    total = terms[half][offset, kind, rows, :]
                    if not fresh:
                        sum_copy(half, direction, step - 1, part).wait_recv()
                        total = total + come[half][direction, step - 1, kind, rows, :].astype(jnp.float32)
                    away[half][direction, step, kind, rows, :] = total.astype(jnp.bfloat16)
                    sum_copy(half, direction, step, part).start()

    for half in (0, 1):
        chunk(half, (0,))
    if most > 2:
        ring_step(most - 1)
    for distance in range(1, most - 1):
        for half in (0, 1):
            if distance < counts[half] // 2 - 1:
                chunk(half, (distance, -distance))
    for half in (0, 1):
        reach = counts[half] // 2
        for direction in (0, 1):
            for part in ring_parts(half, direction, reach - 1):
                ring_copy(half, direction, reach - 1, part, True).wait_recv()
        chunk(half, (reach,))
    sum_step(0, True)
    for half in (0, 1):
        reach = counts[half] // 2
        if reach > 1:
            for direction in (0, 1):
                for piece in range(pieces):
                    ring_copy(half, direction, reach - 2, (1 - direction, piece), True).wait_recv()
            chunk(half, (reach - 1, 1 - reach))
    if most > 1:
        sum_step(1, True)

    def dq_copy(half, target, origin):
        return remote(
            dq_away[half].at[target],
            dq_come[half].at[origin],
            dq_send.at[0],
            dq_recv.at[half, origin],
            peer(1 - half, target),
        )

    for half in (0, 1):
        axis = 1 - half
        full = jnp.transpose(turned[half][...]).reshape(counts[axis], pairs, width)
        dq_full[half][...] = full
        dq_away[half][...] = full.astype(jnp.bfloat16)
        for d in reversed(other_coords(counts[axis])):
            dq_copy(half, around(axis, d), position[axis]).start()

    for step in range(1, most):
        if step > 1:
            sum_step(step, True)
        sum_step(step, False)

    dq_sum = dq_full[0][position[1]] + dq_full[1][position[0]]
    for half in (0, 1):
        axis = 1 - half
        for d in other_coords(counts[axis]):
            j = around(axis, d)
            dq_copy(half, position[axis], j).wait_recv()
            dq_sum = dq_sum + dq_come[half][j].astype(jnp.float32)
    dq_rows = dq_sum * scale
    for group in range(groups):
        back[group] = dq_rows[group * heads : (group + 1) * heads].astype(jnp.bfloat16)

    def back_copy(target, origin):
        return remote(
            back.at[target], back_come.at[origin], back_send.at[0], back_recv.at[origin], (target, place)
        )

    for d in other_coords(groups):
        back_copy(lax.rem(mine + d, groups), mine).start()
    back_come[mine] = back[mine]

    for part in every_part:
        kind, piece = part
        for half in (0, 1):
            last = counts[half] // 2 - 1
            rows = pl.ds(piece * piece_rows, piece_rows)
            total = terms[half][0, kind, rows, :]
            for direction in (0, 1):
                if part in sum_parts(direction, last):
                    sum_copy(half, direction, last, part).wait_recv()
                    total = total + come[half][direction, last, kind, rows, :].astype(jnp.float32)
            result = dvalues_ref if kind else dkeys_ref
            result[pl.ds(half * half_keys + piece * piece_rows, piece_rows), :] = total.astype(jnp.bfloat16)

    for d in range(1, groups):
        back_copy(mine, lax.rem(mine + d, groups)).wait_recv()
    dq_ref[...] = back_come[...]

    for d in range(1, groups):
        target = lax.rem(mine + d, groups)
        for copy in exchange(target, mine):
            copy.wait_send()
        back_copy(target, mine).wait_send()
    for half in (0, 1):
        axis = 1 - half
        for d in range(1, counts[axis]):
            target = around(axis, d)
            for copy in block_copies(half, target, position[axis]):
                copy.wait_send()
            dq_copy(half, target, position[axis]).wait_send()
        for direction in (0, 1):
            for step in range(counts[half] // 2):
                for part in ring_parts(half, direction, step):
                    ring_copy(half, direction, step, part).wait_send()
                for part in sum_parts(direction, step):
                    sum_copy(half, direction, step, part).wait_send()


def store_kernel(dq_ref, dkeys_ref, dvalues_ref, dq_hbm, dkeys_hbm, dvalues_hbm, dq_row, sem):
    copies = [
        pltpu.make_async_copy(dkeys_ref, dkeys_hbm, sem.at[0]),
        pltpu.make_async_copy(dvalues_ref, dvalues_hbm, sem.at[1]),
        pltpu.make_async_copy(dq_row, dq_hbm, sem.at[2]),
    ]
    copies[0].start()
    copies[1].start()
    groups, heads, width = dq_ref.shape
    for group in range(groups):
        rows = dq_ref[group].astype(jnp.float32)
        for head in range(heads):
            first = (group * heads + head) * width
            dq_row[:, first : first + width] = rows[head : head + 1].astype(jnp.bfloat16)
    copies[2].start()
    for copy in copies:
        copy.wait()


def shards(ny, nz, queries, out_grad, saved_out, saved_lse, video_keys, video_values):
    groups = lax.axis_size("kv")
    width = video_keys.shape[1]
    heads = queries.shape[1] // (groups * width)
    key_rows = video_keys.shape[0]
    half_keys = key_rows // 2
    pairs = groups * heads
    counts = (ny, nz)
    bf16, f32 = jnp.bfloat16, jnp.float32
    dma = pltpu.SemaphoreType.DMA
    most = max(counts)
    across = (counts[1], counts[0])
    pieces = 2
    row = groups * heads * width
    scratch = (
        [pltpu.VMEM((1, row), bf16)] * 3
        + [pltpu.VMEM((1, groups * heads), f32)]
        + [
            pltpu.VMEM((groups, 2 * heads, width), bf16),
            pltpu.VMEM((groups, 2 * heads, LANES), f32),
            pltpu.VMEM((groups, 2 * heads, width), bf16),
            pltpu.VMEM((groups, 2 * heads, LANES), f32),
        ]
        + [pltpu.VMEM((n, 2, half_keys, width), bf16) for n in counts]
        + [pltpu.VMEM((n, 2 * pairs, width), bf16) for n in across]
        + [pltpu.VMEM((n, 2, LANES), f32) for n in across]
        + [pltpu.VMEM((n, 2, half_keys, width), f32) for n in counts]
        + [pltpu.VMEM((2, n // 2, 2, half_keys, width), bf16) for n in counts]
        + [pltpu.VMEM((2, n // 2, 2, half_keys, width), bf16) for n in counts]
        + [pltpu.VMEM((width, n * pairs), f32) for n in across]
        + [pltpu.VMEM((n, pairs, width), f32) for n in across]
        + [pltpu.VMEM((n, pairs, width), bf16) for n in across]
        + [pltpu.VMEM((n, pairs, width), bf16) for n in across]
        + [pltpu.VMEM((groups, heads, width), bf16), pltpu.VMEM((groups, heads, width), bf16)]
        + [
            dma((4,)),
            dma((2, 2)),
            dma((1,)),
            dma((groups, 2)),
            dma((1,)),
            dma((2, 2, most // 2, 2 * pieces)),
            dma((1,)),
            dma((2, most, 2)),
            dma((1,)),
            dma((2, 2, most // 2, 2 * pieces)),
            dma((1,)),
            dma((2, most)),
            dma((1,)),
            dma((groups,)),
        ]
    )
    vmem = pl.BlockSpec(memory_space=pltpu.VMEM)
    hbm = pl.BlockSpec(memory_space=pltpu.HBM)
    arguments = (queries, out_grad, saved_out, saved_lse, video_keys, video_values)
    arguments = [pltpu.with_memory_space_constraint(argument, pltpu.HBM) for argument in arguments]
    dq, dkeys, dvalues = pl.pallas_call(
        functools.partial(kernel, (groups, ny, nz, heads, width, half_keys, pieces)),
        out_shape=(
            jax.ShapeDtypeStruct((groups, heads, width), bf16),
            jax.ShapeDtypeStruct((key_rows, width), bf16),
            jax.ShapeDtypeStruct((key_rows, width), bf16),
        ),
        in_specs=[hbm] * 6,
        out_specs=(vmem, vmem, vmem),
        scratch_shapes=scratch,
        compiler_params=pltpu.CompilerParams(
            collective_id=0, has_side_effects=True, vmem_limit_bytes=40 * 1024 * 1024
        ),
        name="attention_backward",
    )(*arguments)
    return pl.pallas_call(
        store_kernel,
        out_shape=(
            jax.ShapeDtypeStruct((1, row), bf16),
            jax.ShapeDtypeStruct((key_rows, width), bf16),
            jax.ShapeDtypeStruct((key_rows, width), bf16),
        ),
        in_specs=[vmem] * 3,
        out_specs=(hbm, hbm, hbm),
        scratch_shapes=[pltpu.VMEM((1, row), bf16), dma((3,))],
        compiler_params=pltpu.CompilerParams(vmem_limit_bytes=1024 * 1024),
        name="store_results",
    )(dq, dkeys, dvalues)


def solution(mesh):
    seq = mesh.shape["seq"]
    ny = 1
    while ny * ny < seq:
        ny *= 2
    nz = seq // ny
    rows = P(("kv", "seq"), None)
    keys = P("seq", "kv")
    return jax.shard_map(
        functools.partial(shards, ny, nz),
        mesh=mesh,
        in_specs=(rows, rows, rows, rows, keys, keys),
        out_specs=(rows, keys, keys),
        check_vma=False,
    )
```

```python
import functools
import math

import jax
import jax.numpy as jnp
from jax import lax
from jax.experimental import pallas as pl
from jax.experimental.pallas import tpu as pltpu
from jax.sharding import PartitionSpec as P

MESH = pl.DeviceIdType.MESH
LANES = 128


def other_coords(count):
    return sorted(range(1, count), key=lambda d: (min(d, count - d), d))


def kernel(
    sizes,
    q_hbm,
    grad_hbm,
    out_hbm,
    lse_hbm,
    keys_ref,
    values_ref,
    dq_ref,
    dkeys_ref,
    dvalues_ref,
    q_ref,
    grad_ref,
    out_ref,
    lse_ref,
    packet,
    packet_aux,
    got,
    got_aux,
    held0,
    held1,
    block0,
    block1,
    aux0,
    aux1,
    terms0,
    terms1,
    away0,
    away1,
    come0,
    come1,
    turned0,
    turned1,
    dq_full0,
    dq_full1,
    dq_away0,
    dq_away1,
    dq_come0,
    dq_come1,
    back,
    back_come,
    row_sem,
    load_sem,
    send_sem,
    exchange_recv,
    near_recv,
    two_recv,
    far_recv,
    block_recv,
    up_recv,
    last_recv,
    dq_recv,
    back_recv,
):
    groups, ny, nz, heads, width, half_keys, pieces = sizes
    piece_rows = half_keys // pieces
    counts = (ny, nz)
    held, block, aux = (held0, held1), (block0, block1), (aux0, aux1)
    terms, away, come = (terms0, terms1), (away0, away1), (come0, come1)
    turned = (turned0, turned1)
    dq_full = (dq_full0, dq_full1)
    dq_away, dq_come = (dq_away0, dq_away1), (dq_come0, dq_come1)
    pairs = groups * heads
    scale = 1.0 / math.sqrt(width)

    mine = lax.axis_index("kv")
    place = lax.axis_index("seq")
    y, z = lax.rem(place, ny), lax.div(place, ny)
    position = (y, z)

    def peer(axis, index):
        return (mine, z * ny + index) if axis == 0 else (mine, index * ny + y)

    def around(axis, step):
        return lax.rem(position[axis] + (step % counts[axis]), counts[axis])

    def remote(src, dst, send, recv, device):
        return pltpu.make_async_remote_copy(
            src_ref=src, dst_ref=dst, send_sem=send, recv_sem=recv, device_id=device, device_id_type=MESH
        )

    def wait_bytes(ref, sem):
        remote(ref, ref, send_sem.at[0], sem, (lax.rem(mine + 1, groups), place)).wait_recv()

    row_loads = []
    for index, (source, target) in enumerate(
        ((q_hbm, q_ref), (grad_hbm, grad_ref), (out_hbm, out_ref), (lse_hbm, lse_ref))
    ):
        copy = pltpu.make_async_copy(source, target, row_sem.at[index])
        copy.start()
        row_loads.append(copy)

    barrier = pltpu.get_barrier_semaphore()
    for d in range(1, groups):
        pl.semaphore_signal(barrier, inc=1, device_id=(lax.rem(mine + d, groups), place), device_id_type=MESH)
    for axis in (0, 1):
        for d in range(1, counts[axis]):
            pl.semaphore_signal(barrier, inc=1, device_id=peer(axis, around(axis, d)), device_id_type=MESH)

    loads = []
    for half in (0, 1):
        for part, source in ((0, keys_ref), (1, values_ref)):
            copy = pltpu.make_async_copy(
                source.at[pl.ds(half * half_keys, half_keys), :],
                held[half].at[position[half], part],
                load_sem.at[half, part],
            )
            copy.start()
            loads.append(copy)

    for copy in row_loads:
        copy.wait()

    def rows_of(ref):
        flat = ref[...].astype(jnp.float32)
        return jnp.concatenate([flat[:, i * width : (i + 1) * width] for i in range(pairs)], axis=0)

    q_rows, grad_rows, out_rows = rows_of(q_ref), rows_of(grad_ref), rows_of(out_ref)
    delta_column = jnp.sum(grad_rows * out_rows, axis=1, keepdims=True)
    eye = lax.broadcasted_iota(jnp.int32, (pairs, pairs), 0) == lax.broadcasted_iota(jnp.int32, (pairs, pairs), 1)
    lse_column = jnp.sum(
        jnp.where(eye, jnp.broadcast_to(lse_ref[...], (pairs, pairs)), 0.0), axis=1, keepdims=True
    )
    lane = lax.broadcasted_iota(jnp.int32, (pairs, LANES), 1)
    member = lax.rem(lax.broadcasted_iota(jnp.int32, (pairs, LANES), 0), heads)
    spot = lane == mine * heads + member
    lse_spots = jnp.where(spot, jnp.broadcast_to(lse_column, (pairs, LANES)), 0.0)
    delta_spots = jnp.where(spot, jnp.broadcast_to(delta_column, (pairs, LANES)), 0.0)
    for group in range(groups):
        rows = slice(group * heads, (group + 1) * heads)
        packet[group] = jnp.concatenate([q_rows[rows], grad_rows[rows]], axis=0).astype(jnp.bfloat16)
        packet_aux[group] = jnp.concatenate([lse_spots[rows], delta_spots[rows]], axis=0)

    pl.semaphore_wait(barrier, groups - 1 + ny - 1 + nz - 1)

    def exchange(target, origin):
        device = (target, place)
        return (
            remote(packet.at[target], got.at[origin], send_sem.at[0], exchange_recv.at[0], device),
            remote(
                packet_aux.at[target],
                got_aux.at[origin],
                send_sem.at[0],
                exchange_recv.at[1],
                device,
            ),
        )

    for d in other_coords(groups):
        for copy in exchange(lax.rem(mine + d, groups), mine):
            copy.start()
    got[mine] = packet[mine]
    got_aux[mine] = packet_aux[mine]

    every_part = [(kind, piece) for kind in (0, 1) for piece in range(pieces)]
    streams = [(axis, direction) for axis in (0, 1) for direction in (0, 1)]

    def farthest(axis):
        return counts[axis] // 2

    def parts_at(axis, direction, distance):
        kinds = (0, 1) if distance < farthest(axis) else (direction,)
        return [(kind, piece) for kind in kinds for piece in range(pieces)]

    def stop(distance):
        return 2 if distance > 2 else 0

    def toward(direction, steps):
        return steps if direction == 0 else -steps

    def gather_copy(axis, direction, distance, part, arriving=False):
        kind, piece = part
        reach = distance if arriving else stop(distance)
        ref = held[axis].at[around(axis, toward(direction, -reach)), kind, pl.ds(piece * piece_rows, piece_rows), :]
        if distance == 1:
            sem = near_recv.at[axis]
        elif distance == 2:
            sem = two_recv.at[axis, direction, kind * pieces + piece]
        else:
            sem = far_recv.at[axis, distance - 3]
        target = peer(axis, around(axis, toward(direction, distance - stop(distance))))
        return remote(ref, ref, send_sem.at[1], sem, target)

    def gather_wait(axis, distance):
        if distance == 2:
            for direction in (0, 1):
                for part in parts_at(axis, direction, distance):
                    gather_copy(axis, direction, distance, part, True).wait_recv()
        else:
            sem = near_recv.at[axis] if distance == 1 else far_recv.at[axis, distance - 3]
            wait_bytes(held[axis].at[pl.ds(0, 2 if distance < farthest(axis) else 1)], sem)

    for copy in loads:
        copy.wait()
    for distance in (2, 1):
        for part in every_part:
            for axis, direction in streams:
                if distance <= farthest(axis) and part in parts_at(axis, direction, distance):
                    gather_copy(axis, direction, distance, part).start()

    wait_bytes(got.at[pl.ds(0, groups - 1)], exchange_recv.at[0])
    wait_bytes(got_aux.at[pl.ds(0, groups - 1)], exchange_recv.at[1])
    got_rows = got[...].astype(jnp.float32)
    own_block = jnp.concatenate(
        [got_rows[i, :heads] for i in range(groups)] + [got_rows[i, heads:] for i in range(groups)], axis=0
    ).astype(jnp.bfloat16)
    got_sum = jnp.sum(got_aux[...], axis=0)
    own_aux = [
        jnp.sum(got_sum[:heads], axis=0, keepdims=True),
        jnp.sum(got_sum[heads:], axis=0, keepdims=True),
    ]
    per_row = LANES // pairs
    lane_row = lax.broadcasted_iota(jnp.int32, (1, LANES), 1)

    def block_copies(half, target, origin):
        axis = 1 - half
        device = peer(axis, target)
        return (
            remote(
                block[half].at[origin],
                block[half].at[origin],
                send_sem.at[2],
                block_recv.at[half, 0],
                device,
            ),
            remote(
                aux[half].at[origin],
                aux[half].at[origin],
                send_sem.at[2],
                block_recv.at[half, 1],
                device,
            ),
        )

    for half in (0, 1):
        at = position[1 - half]
        block[half][at] = own_block
        inside = lax.div(lane_row, pairs) == lax.rem(at, per_row)
        spread = []
        for vector in own_aux:
            total = vector
            for k in range(1, per_row):
                total = total + pltpu.roll(vector, k * pairs, 1)
            spread.append(jnp.where(inside, total, 0.0))
        aux[half][at] = jnp.concatenate(spread, axis=0)
    for half in (0, 1):
        axis = 1 - half
        for d in reversed(other_coords(counts[axis])):
            for copy in block_copies(half, around(axis, d), position[axis]):
                copy.start()

    for part in every_part:
        for axis, direction in streams:
            if farthest(axis) > 2:
                gather_copy(axis, direction, 2, part, True).wait_recv()
                for distance in range(3, farthest(axis) + 1):
                    if part in parts_at(axis, direction, distance):
                        gather_copy(axis, direction, distance, part).start()

    lse_rows, delta_rows = [], []
    for half in (0, 1):
        axis = 1 - half
        wait_bytes(block[half].at[pl.ds(0, counts[axis] - 1)], block_recv.at[half, 0])
        wait_bytes(aux[half].at[pl.ds(0, counts[axis] - 1)], block_recv.at[half, 1])
        total_pairs = counts[axis] * pairs
        for index, found in ((0, lse_rows), (1, delta_rows)):
            sums = []
            for first in range(0, counts[axis], per_row):
                piece = aux[half][first, index : index + 1, :]
                for j in range(first + 1, min(first + per_row, counts[axis])):
                    piece = piece + aux[half][j, index : index + 1, :]
                sums.append(piece)
            found.append(jnp.concatenate(sums, axis=1)[:, :total_pairs])
        turned[half][...] = jnp.zeros_like(turned[half])

    def chunk(half, offsets):
        total_pairs = counts[1 - half] * pairs
        q_all = block[half][:, :pairs, :].reshape(total_pairs, width)
        grad_all = block[half][:, pairs:, :].reshape(total_pairs, width)
        places = [around(half, offset) for offset in offsets]
        key = jnp.concatenate([held[half][at, 0] for at in places], axis=0)
        value = jnp.concatenate([held[half][at, 1] for at in places], axis=0)
        across = (((1,), (1,)), ((), ()))
        scores = lax.dot_general(key, q_all, across, preferred_element_type=jnp.float32)
        probs = jnp.exp(scores * scale - lse_rows[half])
        dprobs = lax.dot_general(value, grad_all, across, preferred_element_type=jnp.float32)
        dscores = (probs * (dprobs - delta_rows[half])).astype(jnp.bfloat16)
        dvalue = jnp.dot(probs.astype(jnp.bfloat16), grad_all, preferred_element_type=jnp.float32)
        dkey = jnp.dot(dscores, q_all, preferred_element_type=jnp.float32) * scale
        turned[half][...] += lax.dot_general(
            key, dscores, (((0,), (0,)), ((), ())), preferred_element_type=jnp.float32
        )
        for index, offset in enumerate(offsets):
            rows = slice(index * half_keys, (index + 1) * half_keys)
            terms[half][offset % counts[half], 0] = dkey[rows]
            terms[half][offset % counts[half], 1] = dvalue[rows]

    def sum_copy(axis, direction, distance, part):
        kind, piece = part
        rows = pl.ds(piece * piece_rows, piece_rows)
        if distance > 2:
            sem = up_recv.at[axis, direction, distance - 3, kind * pieces + piece]
        else:
            sem = last_recv.at[axis, distance - 1]
        return remote(
            away[axis].at[direction, distance - 1, kind, rows, :],
            come[axis].at[direction, distance - 1, kind, rows, :],
            send_sem.at[3],
            sem,
            peer(axis, around(axis, toward(direction, distance - stop(distance)))),
        )

    def sum_send(distance, axes=(0, 1)):
        for part in every_part:
            kind, piece = part
            rows = pl.ds(piece * piece_rows, piece_rows)
            for axis, direction in streams:
                if axis not in axes or distance > farthest(axis) or part not in parts_at(axis, direction, distance):
                    continue
                total = terms[axis][toward(direction, distance) % counts[axis], kind, rows, :]
                if distance == 2:
                    for beyond in range(3, farthest(axis) + 1):
                        if part in parts_at(axis, direction, beyond):
                            sum_copy(axis, direction, beyond, part).wait_recv()
                            total = total + come[axis][direction, beyond - 1, kind, rows, :].astype(jnp.float32)
                away[axis][direction, distance - 1, kind, rows, :] = total.astype(jnp.bfloat16)
                sum_copy(axis, direction, distance, part).start()

    most = max(counts) // 2
    for half in (0, 1):
        chunk(half, (0,))
    for distance in range(1, most - 1):
        for half in (0, 1):
            if distance < farthest(half) - 1:
                if distance == 1:
                    gather_wait(half, 1)
                chunk(half, (distance, -distance))
    sum_send(1, [axis for axis in (0, 1) if farthest(axis) > 2])
    for half in (0, 1):
        gather_wait(half, farthest(half))
        chunk(half, (farthest(half),))
    if most > 2:
        sum_send(most)
    for half in (0, 1):
        before = farthest(half) - 1
        if before > 0:
            gather_wait(half, before)
            chunk(half, (before, -before))
    for distance in range(most - 1, 2, -1):
        sum_send(distance)

    def dq_copy(half, target, origin):
        return remote(
            dq_away[half].at[target],
            dq_come[half].at[origin],
            send_sem.at[4],
            dq_recv.at[half],
            peer(1 - half, target),
        )

    for half in (0, 1):
        axis = 1 - half
        full = jnp.transpose(turned[half][...]).reshape(counts[axis], pairs, width)
        dq_full[half][...] = full
        dq_away[half][...] = full.astype(jnp.bfloat16)
        for d in reversed(other_coords(counts[axis])):
            dq_copy(half, around(axis, d), position[axis]).start()

    sum_send(1, [axis for axis in (0, 1) if farthest(axis) <= 2])
    sum_send(2)

    for half in (0, 1):
        axis = 1 - half
        wait_bytes(dq_come[half].at[pl.ds(0, counts[axis] - 1)], dq_recv.at[half])
    dq_sum = dq_full[0][position[1]] + dq_full[1][position[0]]
    for half in (0, 1):
        axis = 1 - half
        for d in range(1, counts[axis]):
            dq_sum = dq_sum + dq_come[half][around(axis, d)].astype(jnp.float32)
    dq_rows = dq_sum * scale
    for group in range(groups):
        back[group] = dq_rows[group * heads : (group + 1) * heads].astype(jnp.bfloat16)

    def back_copy(target, origin):
        return remote(
            back.at[target], back_come.at[origin], send_sem.at[5], back_recv.at[0], (target, place)
        )

    for d in other_coords(groups):
        back_copy(lax.rem(mine + d, groups), mine).start()
    back_come[mine] = back[mine]

    for axis in (0, 1):
        for distance in range(1, min(2, farthest(axis)) + 1):
            whole = come[axis].at[:, distance - 1] if distance < farthest(axis) else come[axis].at[0, distance - 1]
            wait_bytes(whole, last_recv.at[axis, distance - 1])
    for half in (0, 1):
        for kind, result in ((0, dkeys_ref), (1, dvalues_ref)):
            total = terms[half][0, kind]
            for direction in (0, 1):
                for distance in (1, 2):
                    if distance <= farthest(half) and (kind, 0) in parts_at(half, direction, distance):
                        total = total + come[half][direction, distance - 1, kind].astype(jnp.float32)
            result[pl.ds(half * half_keys, half_keys), :] = total.astype(jnp.bfloat16)

    wait_bytes(back_come.at[pl.ds(0, groups - 1)], back_recv.at[0])
    dq_ref[...] = back_come[...]

    for d in range(1, groups):
        target = lax.rem(mine + d, groups)
        for copy in exchange(target, mine):
            copy.wait_send()
        back_copy(target, mine).wait_send()
    for half in (0, 1):
        axis = 1 - half
        for d in range(1, counts[axis]):
            target = around(axis, d)
            for copy in block_copies(half, target, position[axis]):
                copy.wait_send()
            dq_copy(half, target, position[axis]).wait_send()
        for direction in (0, 1):
            for distance in range(1, farthest(half) + 1):
                for part in parts_at(half, direction, distance):
                    gather_copy(half, direction, distance, part).wait_send()
                    sum_copy(half, direction, distance, part).wait_send()


def store_kernel(dq_ref, dkeys_ref, dvalues_ref, dq_hbm, dkeys_hbm, dvalues_hbm, dq_row, sem):
    copies = [
        pltpu.make_async_copy(dkeys_ref, dkeys_hbm, sem.at[0]),
        pltpu.make_async_copy(dvalues_ref, dvalues_hbm, sem.at[1]),
        pltpu.make_async_copy(dq_row, dq_hbm, sem.at[2]),
    ]
    copies[0].start()
    copies[1].start()
    groups, heads, width = dq_ref.shape
    for group in range(groups):
        rows = dq_ref[group].astype(jnp.float32)
        for head in range(heads):
            first = (group * heads + head) * width
            dq_row[:, first : first + width] = rows[head : head + 1].astype(jnp.bfloat16)
    copies[2].start()
    for copy in copies:
        copy.wait()


def shards(ny, nz, queries, out_grad, saved_out, saved_lse, video_keys, video_values):
    groups = lax.axis_size("kv")
    width = video_keys.shape[1]
    heads = queries.shape[1] // (groups * width)
    key_rows = video_keys.shape[0]
    half_keys = key_rows // 2
    pairs = groups * heads
    counts = (ny, nz)
    bf16, f32 = jnp.bfloat16, jnp.float32
    dma = pltpu.SemaphoreType.DMA
    across = (counts[1], counts[0])
    pieces = 2
    row = groups * heads * width
    scratch = (
        [pltpu.VMEM((1, row), bf16)] * 3
        + [pltpu.VMEM((1, groups * heads), f32)]
        + [
            pltpu.VMEM((groups, 2 * heads, width), bf16),
            pltpu.VMEM((groups, 2 * heads, LANES), f32),
            pltpu.VMEM((groups, 2 * heads, width), bf16),
            pltpu.VMEM((groups, 2 * heads, LANES), f32),
        ]
        + [pltpu.VMEM((n, 2, half_keys, width), bf16) for n in counts]
        + [pltpu.VMEM((n, 2 * pairs, width), bf16) for n in across]
        + [pltpu.VMEM((n, 2, LANES), f32) for n in across]
        + [pltpu.VMEM((n, 2, half_keys, width), f32) for n in counts]
        + [pltpu.VMEM((2, n // 2, 2, half_keys, width), bf16) for n in counts]
        + [pltpu.VMEM((2, n // 2, 2, half_keys, width), bf16) for n in counts]
        + [pltpu.VMEM((width, n * pairs), f32) for n in across]
        + [pltpu.VMEM((n, pairs, width), f32) for n in across]
        + [pltpu.VMEM((n, pairs, width), bf16) for n in across]
        + [pltpu.VMEM((n, pairs, width), bf16) for n in across]
        + [pltpu.VMEM((groups, heads, width), bf16), pltpu.VMEM((groups, heads, width), bf16)]
        + [
            dma((4,)),
            dma((2, 2)),
            dma((6,)),
            dma((2,)),
            dma((2,)),
            dma((2, 2, 2 * pieces)),
            dma((2, 2)),
            dma((2, 2)),
            dma((2, 2, 2, 2 * pieces)),
            dma((2, 2)),
            dma((2,)),
            dma((1,)),
        ]
    )
    vmem = pl.BlockSpec(memory_space=pltpu.VMEM)
    hbm = pl.BlockSpec(memory_space=pltpu.HBM)
    arguments = (queries, out_grad, saved_out, saved_lse, video_keys, video_values)
    arguments = [pltpu.with_memory_space_constraint(argument, pltpu.HBM) for argument in arguments]
    dq, dkeys, dvalues = pl.pallas_call(
        functools.partial(kernel, (groups, ny, nz, heads, width, half_keys, pieces)),
        out_shape=(
            jax.ShapeDtypeStruct((groups, heads, width), bf16),
            jax.ShapeDtypeStruct((key_rows, width), bf16),
            jax.ShapeDtypeStruct((key_rows, width), bf16),
        ),
        in_specs=[hbm] * 6,
        out_specs=(vmem, vmem, vmem),
        scratch_shapes=scratch,
        compiler_params=pltpu.CompilerParams(
            collective_id=0, has_side_effects=True, vmem_limit_bytes=40 * 1024 * 1024
        ),
        name="attention_backward",
    )(*arguments)
    return pl.pallas_call(
        store_kernel,
        out_shape=(
            jax.ShapeDtypeStruct((1, row), bf16),
            jax.ShapeDtypeStruct((key_rows, width), bf16),
            jax.ShapeDtypeStruct((key_rows, width), bf16),
        ),
        in_specs=[vmem] * 3,
        out_specs=(hbm, hbm, hbm),
        scratch_shapes=[pltpu.VMEM((1, row), bf16), dma((3,))],
        compiler_params=pltpu.CompilerParams(vmem_limit_bytes=1024 * 1024),
        name="store_results",
    )(dq, dkeys, dvalues)


def solution(mesh):
    seq = mesh.shape["seq"]
    ny = 1
    while ny * ny < seq:
        ny *= 2
    nz = seq // ny
    rows = P(("kv", "seq"), None)
    keys = P("seq", "kv")
    return jax.shard_map(
        functools.partial(shards, ny, nz),
        mesh=mesh,
        in_specs=(rows, rows, rows, rows, keys, keys),
        out_specs=(rows, keys, keys),
        check_vma=False,
    )
```

```python
import functools
import math

import jax
import jax.numpy as jnp
from jax import lax
from jax.experimental import pallas as pl
from jax.experimental.pallas import tpu as pltpu
from jax.sharding import PartitionSpec as P

MESH = pl.DeviceIdType.MESH
LANES = 128


def other_coords(count):
    return sorted(range(1, count), key=lambda d: (min(d, count - d), d))


def near_offsets(count):
    return [d for d in range(1, count) if min(d, count - d) <= 2]


def kernel(
    sizes,
    q_hbm,
    grad_hbm,
    out_hbm,
    lse_hbm,
    keys_ref,
    values_ref,
    dq_ref,
    dkeys_ref,
    dvalues_ref,
    q_ref,
    grad_ref,
    out_ref,
    lse_ref,
    packet,
    packet_aux,
    got,
    got_aux,
    held0,
    held1,
    block0,
    block1,
    aux0,
    aux1,
    terms0,
    terms1,
    away0,
    away1,
    come0,
    come1,
    turned0,
    turned1,
    dq_full0,
    dq_full1,
    dq_away0,
    dq_away1,
    dq_come0,
    dq_come1,
    back,
    row_sem,
    load_sem,
    entered,
    send_sem,
    exchange_recv,
    near_recv,
    two_recv,
    far_recv,
    block_recv,
    up_recv,
    last_recv,
    dq_recv,
    back_recv,
):
    groups, ny, nz, heads, width, half_keys, pieces = sizes
    piece_rows = half_keys // pieces
    counts = (ny, nz)
    held, block, aux = (held0, held1), (block0, block1), (aux0, aux1)
    terms, away, come = (terms0, terms1), (away0, away1), (come0, come1)
    turned = (turned0, turned1)
    dq_full = (dq_full0, dq_full1)
    dq_away, dq_come = (dq_away0, dq_away1), (dq_come0, dq_come1)
    pairs = groups * heads
    scale = 1.0 / math.sqrt(width)

    mine = lax.axis_index("kv")
    place = lax.axis_index("seq")
    y, z = lax.rem(place, ny), lax.div(place, ny)
    position = (y, z)

    def peer(axis, index):
        return (mine, z * ny + index) if axis == 0 else (mine, index * ny + y)

    def around(axis, step):
        return lax.rem(position[axis] + (step % counts[axis]), counts[axis])

    def remote(src, dst, send, recv, device):
        return pltpu.make_async_remote_copy(
            src_ref=src, dst_ref=dst, send_sem=send, recv_sem=recv, device_id=device, device_id_type=MESH
        )

    def wait_bytes(ref, sem):
        remote(ref, ref, send_sem.at[0], sem, (lax.rem(mine + 1, groups), place)).wait_recv()

    row_loads = []
    for index, (source, target) in enumerate(
        ((q_hbm, q_ref), (grad_hbm, grad_ref), (out_hbm, out_ref), (lse_hbm, lse_ref))
    ):
        copy = pltpu.make_async_copy(source, target, row_sem.at[index])
        copy.start()
        row_loads.append(copy)

    barrier = pltpu.get_barrier_semaphore()
    for d in range(1, groups):
        pl.semaphore_signal(barrier, inc=1, device_id=(lax.rem(mine + d, groups), place), device_id_type=MESH)
    for axis in (0, 1):
        for d in near_offsets(counts[axis]):
            pl.semaphore_signal(barrier, inc=1, device_id=peer(axis, around(axis, d)), device_id_type=MESH)

    loads = []
    for half in (0, 1):
        for part, source in ((0, keys_ref), (1, values_ref)):
            copy = pltpu.make_async_copy(
                source.at[pl.ds(half * half_keys, half_keys), :],
                held[half].at[position[half], part],
                load_sem.at[half, part],
            )
            copy.start()
            loads.append(copy)

    for copy in row_loads:
        copy.wait()

    def rows_of(ref):
        flat = ref[...].astype(jnp.float32)
        return jnp.concatenate([flat[:, i * width : (i + 1) * width] for i in range(pairs)], axis=0)

    q_rows, grad_rows, out_rows = rows_of(q_ref), rows_of(grad_ref), rows_of(out_ref)
    delta_column = jnp.sum(grad_rows * out_rows, axis=1, keepdims=True)
    eye = lax.broadcasted_iota(jnp.int32, (pairs, pairs), 0) == lax.broadcasted_iota(jnp.int32, (pairs, pairs), 1)
    lse_column = jnp.sum(
        jnp.where(eye, jnp.broadcast_to(lse_ref[...], (pairs, pairs)), 0.0), axis=1, keepdims=True
    )
    lane = lax.broadcasted_iota(jnp.int32, (pairs, LANES), 1)
    member = lax.rem(lax.broadcasted_iota(jnp.int32, (pairs, LANES), 0), heads)
    spot = lane == mine * heads + member
    lse_spots = jnp.where(spot, jnp.broadcast_to(lse_column, (pairs, LANES)), 0.0)
    delta_spots = jnp.where(spot, jnp.broadcast_to(delta_column, (pairs, LANES)), 0.0)
    for group in range(groups):
        rows = slice(group * heads, (group + 1) * heads)
        packet[group] = jnp.concatenate([q_rows[rows], grad_rows[rows]], axis=0).astype(jnp.bfloat16)
        packet_aux[group] = jnp.concatenate([lse_spots[rows], delta_spots[rows]], axis=0)

    pl.semaphore_wait(barrier, groups - 1 + len(near_offsets(ny)) + len(near_offsets(nz)))
    relayed = 0
    for axis in (0, 1):
        if counts[axis] > 5:
            relayed += 2
            for d in (2, -2):
                pl.semaphore_signal(entered, inc=1, device_id=peer(axis, around(axis, d)), device_id_type=MESH)

    def exchange(target, origin):
        device = (target, place)
        return (
            remote(packet.at[target], got.at[origin], send_sem.at[0], exchange_recv.at[0], device),
            remote(
                packet_aux.at[target],
                got_aux.at[origin],
                send_sem.at[0],
                exchange_recv.at[1],
                device,
            ),
        )

    for d in other_coords(groups):
        for copy in exchange(lax.rem(mine + d, groups), mine):
            copy.start()
    got[mine] = packet[mine]
    got_aux[mine] = packet_aux[mine]

    every_part = [(kind, piece) for kind in (0, 1) for piece in range(pieces)]
    streams = [(axis, direction) for axis in (0, 1) for direction in (0, 1)]

    def farthest(axis):
        return counts[axis] // 2

    def parts_at(axis, direction, distance):
        kinds = (0, 1) if distance < farthest(axis) else (direction,)
        return [(kind, piece) for kind in kinds for piece in range(pieces)]

    def stop(distance):
        return 2 if distance > 2 else 0

    def toward(direction, steps):
        return steps if direction == 0 else -steps

    def gather_copy(axis, direction, distance, part, arriving=False):
        kind, piece = part
        reach = distance if arriving else stop(distance)
        ref = held[axis].at[around(axis, toward(direction, -reach)), kind, pl.ds(piece * piece_rows, piece_rows), :]
        if distance == 1:
            sem = near_recv.at[axis]
        elif distance == 2:
            sem = two_recv.at[axis, direction, kind * pieces + piece]
        else:
            sem = far_recv.at[axis, distance - 3]
        target = peer(axis, around(axis, toward(direction, distance - stop(distance))))
        return remote(ref, ref, send_sem.at[1], sem, target)

    def gather_wait(axis, distance):
        if distance == 2:
            for direction in (0, 1):
                for part in parts_at(axis, direction, distance):
                    gather_copy(axis, direction, distance, part, True).wait_recv()
        else:
            sem = near_recv.at[axis] if distance == 1 else far_recv.at[axis, distance - 3]
            wait_bytes(held[axis].at[pl.ds(0, 2 if distance < farthest(axis) else 1)], sem)

    for copy in loads:
        copy.wait()
    for distance in (2, 1):
        for part in every_part:
            for axis, direction in streams:
                if distance <= farthest(axis) and part in parts_at(axis, direction, distance):
                    gather_copy(axis, direction, distance, part).start()

    wait_bytes(got.at[pl.ds(0, groups - 1)], exchange_recv.at[0])
    wait_bytes(got_aux.at[pl.ds(0, groups - 1)], exchange_recv.at[1])
    if relayed:
        pl.semaphore_wait(entered, relayed)
    got_rows = got[...].astype(jnp.float32)
    own_block = jnp.concatenate(
        [got_rows[i, :heads] for i in range(groups)] + [got_rows[i, heads:] for i in range(groups)], axis=0
    ).astype(jnp.bfloat16)
    got_sum = jnp.sum(got_aux[...], axis=0)
    own_aux = [
        jnp.sum(got_sum[:heads], axis=0, keepdims=True),
        jnp.sum(got_sum[heads:], axis=0, keepdims=True),
    ]
    per_row = LANES // pairs
    lane_row = lax.broadcasted_iota(jnp.int32, (1, LANES), 1)

    def block_copies(half, target, origin):
        axis = 1 - half
        device = peer(axis, target)
        return (
            remote(
                block[half].at[origin],
                block[half].at[origin],
                send_sem.at[2],
                block_recv.at[half, 0],
                device,
            ),
            remote(
                aux[half].at[origin],
                aux[half].at[origin],
                send_sem.at[2],
                block_recv.at[half, 1],
                device,
            ),
        )

    for half in (0, 1):
        at = position[1 - half]
        block[half][at] = own_block
        inside = lax.div(lane_row, pairs) == lax.rem(at, per_row)
        spread = []
        for vector in own_aux:
            total = vector
            for k in range(1, per_row):
                total = total + pltpu.roll(vector, k * pairs, 1)
            spread.append(jnp.where(inside, total, 0.0))
        aux[half][at] = jnp.concatenate(spread, axis=0)
    for half in (0, 1):
        axis = 1 - half
        for d in reversed(other_coords(counts[axis])):
            for copy in block_copies(half, around(axis, d), position[axis]):
                copy.start()

    for part in every_part:
        for axis, direction in streams:
            if farthest(axis) > 2:
                gather_copy(axis, direction, 2, part, True).wait_recv()
                for distance in range(3, farthest(axis) + 1):
                    if part in parts_at(axis, direction, distance):
                        gather_copy(axis, direction, distance, part).start()

    lse_rows, delta_rows = [], []
    for half in (0, 1):
        axis = 1 - half
        wait_bytes(block[half].at[pl.ds(0, counts[axis] - 1)], block_recv.at[half, 0])
        wait_bytes(aux[half].at[pl.ds(0, counts[axis] - 1)], block_recv.at[half, 1])
        total_pairs = counts[axis] * pairs
        for index, found in ((0, lse_rows), (1, delta_rows)):
            sums = []
            for first in range(0, counts[axis], per_row):
                piece = aux[half][first, index : index + 1, :]
                for j in range(first + 1, min(first + per_row, counts[axis])):
                    piece = piece + aux[half][j, index : index + 1, :]
                sums.append(piece)
            found.append(jnp.concatenate(sums, axis=1)[:, :total_pairs])
        turned[half][...] = jnp.zeros_like(turned[half])

    def chunks(work):
        across, down = (((1,), (1,)), ((), ())), (((0,), (0,)), ((), ()))
        staged = []
        for half, offsets in work:
            total_pairs = counts[1 - half] * pairs
            q_all = block[half][:, :pairs, :].reshape(total_pairs, width)
            grad_all = block[half][:, pairs:, :].reshape(total_pairs, width)
            places = [around(half, offset) for offset in offsets]
            key = jnp.concatenate([held[half][at, 0] for at in places], axis=0)
            value = jnp.concatenate([held[half][at, 1] for at in places], axis=0)
            scores = lax.dot_general(key, q_all, across, preferred_element_type=jnp.float32)
            dprobs = lax.dot_general(value, grad_all, across, preferred_element_type=jnp.float32)
            staged.append((key, q_all, grad_all, scores, dprobs))
        rounded = []
        for (half, _), (_, _, _, scores, dprobs) in zip(work, staged):
            probs = jnp.exp(scores * scale - lse_rows[half])
            dscores = (probs * (dprobs - delta_rows[half])).astype(jnp.bfloat16)
            rounded.append((probs.astype(jnp.bfloat16), dscores))
        for (half, offsets), (key, q_all, grad_all, _, _), (probs, dscores) in zip(work, staged, rounded):
            dvalue = jnp.dot(probs, grad_all, preferred_element_type=jnp.float32)
            dkey = jnp.dot(dscores, q_all, preferred_element_type=jnp.float32) * scale
            turned[half][...] += lax.dot_general(key, dscores, down, preferred_element_type=jnp.float32)
            for index, offset in enumerate(offsets):
                rows = slice(index * half_keys, (index + 1) * half_keys)
                terms[half][offset % counts[half], 0] = dkey[rows]
                terms[half][offset % counts[half], 1] = dvalue[rows]

    def sum_copy(axis, direction, distance, part):
        kind, piece = part
        rows = pl.ds(piece * piece_rows, piece_rows)
        if distance > 2:
            sem = up_recv.at[axis, direction, distance - 3, kind * pieces + piece]
        else:
            sem = last_recv.at[axis, distance - 1]
        return remote(
            away[axis].at[direction, distance - 1, kind, rows, :],
            come[axis].at[direction, distance - 1, kind, rows, :],
            send_sem.at[3],
            sem,
            peer(axis, around(axis, toward(direction, distance - stop(distance)))),
        )

    def sum_send(distance, axes=(0, 1)):
        for part in every_part:
            kind, piece = part
            rows = pl.ds(piece * piece_rows, piece_rows)
            for axis, direction in streams:
                if axis not in axes or distance > farthest(axis) or part not in parts_at(axis, direction, distance):
                    continue
                total = terms[axis][toward(direction, distance) % counts[axis], kind, rows, :]
                if distance == 2:
                    for beyond in range(3, farthest(axis) + 1):
                        if part in parts_at(axis, direction, beyond):
                            sum_copy(axis, direction, beyond, part).wait_recv()
                            total = total + come[axis][direction, beyond - 1, kind, rows, :].astype(jnp.float32)
                away[axis][direction, distance - 1, kind, rows, :] = total.astype(jnp.bfloat16)
                sum_copy(axis, direction, distance, part).start()

    most = max(counts) // 2
    long_axes = [axis for axis in (0, 1) if farthest(axis) > 2]
    for half in long_axes:
        gather_wait(half, 1)
    chunks([(half, (1, -1)) for half in long_axes])
    sum_send(1, long_axes)
    chunks([(half, (0, 2, -2) if farthest(half) > 3 else (0,)) for half in (0, 1)])
    for half in (0, 1):
        gather_wait(half, farthest(half))
    chunks([(half, (farthest(half),)) for half in (0, 1)])
    if most > 2:
        sum_send(most)
    before = [(half, (farthest(half) - 1, 1 - farthest(half))) for half in (0, 1) if farthest(half) > 1]
    for half, offsets in before:
        gather_wait(half, offsets[0])
    chunks(before)
    for distance in range(most - 1, 2, -1):
        sum_send(distance)

    def dq_copy(half, index, group):
        axis = 1 - half
        return remote(
            dq_away[half].at[index, group],
            dq_come[half].at[position[axis], mine],
            send_sem.at[4],
            dq_recv.at[half],
            (group, peer(axis, index)[1]),
        )

    for half in (0, 1):
        axis = 1 - half
        full = jnp.transpose(turned[half][...])
        dq_full[half][...] = full.reshape(counts[axis], pairs, width)
        for index in range(counts[axis]):
            for group in range(groups):
                first = index * pairs + group * heads
                dq_away[half][index, group] = full[first : first + heads].astype(jnp.bfloat16)
        for d in reversed(other_coords(counts[axis])):
            for group in range(groups):
                dq_copy(half, around(axis, d), group).start()

    def back_copy(group):
        return remote(
            back.at[group], dq_come[0].at[position[1], mine], send_sem.at[5], back_recv.at[0], (group, place)
        )

    own_terms = dq_full[0][position[1]] + dq_full[1][position[0]]
    for group in range(groups):
        back[group] = own_terms[group * heads : (group + 1) * heads].astype(jnp.bfloat16)
    for d in other_coords(groups):
        back_copy(lax.rem(mine + d, groups)).start()
    dq_come[0][position[1], mine] = back[mine]

    sum_send(1, [axis for axis in (0, 1) if axis not in long_axes])
    sum_send(2)

    for half in (0, 1):
        axis = 1 - half
        wait_bytes(dq_come[half].at[pl.ds(0, counts[axis] - 1)], dq_recv.at[half])
    wait_bytes(dq_come[0].at[0, pl.ds(0, groups - 1)], back_recv.at[0])
    dq_sum = dq_come[0][position[1]].astype(jnp.float32)
    for half in (0, 1):
        axis = 1 - half
        for d in range(1, counts[axis]):
            dq_sum = dq_sum + dq_come[half][around(axis, d)].astype(jnp.float32)
    dq_ref[...] = (dq_sum * scale).astype(jnp.bfloat16)

    for axis in (0, 1):
        for distance in range(1, min(2, farthest(axis)) + 1):
            whole = come[axis].at[:, distance - 1] if distance < farthest(axis) else come[axis].at[0, distance - 1]
            wait_bytes(whole, last_recv.at[axis, distance - 1])
    for half in (0, 1):
        for kind, result in ((0, dkeys_ref), (1, dvalues_ref)):
            total = terms[half][0, kind]
            for direction in (0, 1):
                for distance in (1, 2):
                    if distance <= farthest(half) and (kind, 0) in parts_at(half, direction, distance):
                        total = total + come[half][direction, distance - 1, kind].astype(jnp.float32)
            result[pl.ds(half * half_keys, half_keys), :] = total.astype(jnp.bfloat16)

    for d in range(1, groups):
        target = lax.rem(mine + d, groups)
        for copy in exchange(target, mine):
            copy.wait_send()
        back_copy(target).wait_send()
    for half in (0, 1):
        axis = 1 - half
        sent = dq_away[half].at[pl.ds(0, counts[axis] - 1)]
        remote(sent, sent, send_sem.at[4], dq_recv.at[half], (lax.rem(mine + 1, groups), place)).wait_send()
        for d in range(1, counts[axis]):
            target = around(axis, d)
            for copy in block_copies(half, target, position[axis]):
                copy.wait_send()
        for direction in (0, 1):
            for distance in range(1, farthest(half) + 1):
                for part in parts_at(half, direction, distance):
                    gather_copy(half, direction, distance, part).wait_send()
                    sum_copy(half, direction, distance, part).wait_send()


def store_kernel(dq_ref, dkeys_ref, dvalues_ref, dq_hbm, dkeys_hbm, dvalues_hbm, dq_row, sem):
    copies = [
        pltpu.make_async_copy(dkeys_ref, dkeys_hbm, sem.at[0]),
        pltpu.make_async_copy(dvalues_ref, dvalues_hbm, sem.at[1]),
        pltpu.make_async_copy(dq_row, dq_hbm, sem.at[2]),
    ]
    copies[0].start()
    copies[1].start()
    groups, heads, width = dq_ref.shape
    for group in range(groups):
        rows = dq_ref[group].astype(jnp.float32)
        for head in range(heads):
            first = (group * heads + head) * width
            dq_row[:, first : first + width] = rows[head : head + 1].astype(jnp.bfloat16)
    copies[2].start()
    for copy in copies:
        copy.wait()


def shards(ny, nz, queries, out_grad, saved_out, saved_lse, video_keys, video_values):
    groups = lax.axis_size("kv")
    width = video_keys.shape[1]
    heads = queries.shape[1] // (groups * width)
    key_rows = video_keys.shape[0]
    half_keys = key_rows // 2
    pairs = groups * heads
    counts = (ny, nz)
    bf16, f32 = jnp.bfloat16, jnp.float32
    dma = pltpu.SemaphoreType.DMA
    across = (counts[1], counts[0])
    pieces = 2
    row = groups * heads * width
    scratch = (
        [pltpu.VMEM((1, row), bf16)] * 3
        + [pltpu.VMEM((1, groups * heads), f32)]
        + [
            pltpu.VMEM((groups, 2 * heads, width), bf16),
            pltpu.VMEM((groups, 2 * heads, LANES), f32),
            pltpu.VMEM((groups, 2 * heads, width), bf16),
            pltpu.VMEM((groups, 2 * heads, LANES), f32),
        ]
        + [pltpu.VMEM((n, 2, half_keys, width), bf16) for n in counts]
        + [pltpu.VMEM((n, 2 * pairs, width), bf16) for n in across]
        + [pltpu.VMEM((n, 2, LANES), f32) for n in across]
        + [pltpu.VMEM((n, 2, half_keys, width), f32) for n in counts]
        + [pltpu.VMEM((2, n // 2, 2, half_keys, width), bf16) for n in counts]
        + [pltpu.VMEM((2, n // 2, 2, half_keys, width), bf16) for n in counts]
        + [pltpu.VMEM((width, n * pairs), f32) for n in across]
        + [pltpu.VMEM((n, pairs, width), f32) for n in across]
        + [pltpu.VMEM((n, groups, heads, width), bf16) for n in across]
        + [pltpu.VMEM((n, groups, heads, width), bf16) for n in across]
        + [pltpu.VMEM((groups, heads, width), bf16)]
        + [
            dma((4,)),
            dma((2, 2)),
            pltpu.SemaphoreType.REGULAR,
            dma((6,)),
            dma((2,)),
            dma((2,)),
            dma((2, 2, 2 * pieces)),
            dma((2, 2)),
            dma((2, 2)),
            dma((2, 2, 2, 2 * pieces)),
            dma((2, 2)),
            dma((2,)),
            dma((1,)),
        ]
    )
    vmem = pl.BlockSpec(memory_space=pltpu.VMEM)
    hbm = pl.BlockSpec(memory_space=pltpu.HBM)
    arguments = (queries, out_grad, saved_out, saved_lse, video_keys, video_values)
    arguments = [pltpu.with_memory_space_constraint(argument, pltpu.HBM) for argument in arguments]
    dq, dkeys, dvalues = pl.pallas_call(
        functools.partial(kernel, (groups, ny, nz, heads, width, half_keys, pieces)),
        out_shape=(
            jax.ShapeDtypeStruct((groups, heads, width), bf16),
            jax.ShapeDtypeStruct((key_rows, width), bf16),
            jax.ShapeDtypeStruct((key_rows, width), bf16),
        ),
        in_specs=[hbm] * 6,
        out_specs=(vmem, vmem, vmem),
        scratch_shapes=scratch,
        compiler_params=pltpu.CompilerParams(
            collective_id=0, has_side_effects=True, vmem_limit_bytes=40 * 1024 * 1024
        ),
        name="attention_backward",
    )(*arguments)
    return pl.pallas_call(
        store_kernel,
        out_shape=(
            jax.ShapeDtypeStruct((1, row), bf16),
            jax.ShapeDtypeStruct((key_rows, width), bf16),
            jax.ShapeDtypeStruct((key_rows, width), bf16),
        ),
        in_specs=[vmem] * 3,
        out_specs=(hbm, hbm, hbm),
        scratch_shapes=[pltpu.VMEM((1, row), bf16), dma((3,))],
        compiler_params=pltpu.CompilerParams(vmem_limit_bytes=1024 * 1024),
        name="store_results",
    )(dq, dkeys, dvalues)


def solution(mesh):
    seq = mesh.shape["seq"]
    ny = 1
    while ny * ny < seq:
        ny *= 2
    nz = seq // ny
    rows = P(("kv", "seq"), None)
    keys = P("seq", "kv")
    return jax.shard_map(
        functools.partial(shards, ny, nz),
        mesh=mesh,
        in_specs=(rows, rows, rows, rows, keys, keys),
        out_specs=(rows, keys, keys),
        check_vma=False,
    )
```

```python
import functools
import math

import jax
import jax.numpy as jnp
from jax import lax
from jax.experimental import pallas as pl
from jax.experimental.pallas import tpu as pltpu
from jax.sharding import PartitionSpec as P

MESH = pl.DeviceIdType.MESH
LANES = 128


def other_coords(count):
    return sorted(range(1, count), key=lambda d: (min(d, count - d), d))


def near_offsets(count):
    return [d for d in range(1, count) if min(d, count - d) <= 2]


def kernel(
    sizes,
    q_hbm,
    grad_hbm,
    out_hbm,
    lse_hbm,
    keys_ref,
    values_ref,
    dq_ref,
    dkeys_ref,
    dvalues_ref,
    q_ref,
    grad_ref,
    out_ref,
    lse_ref,
    packet,
    packet_aux,
    got,
    got_aux,
    held0,
    held1,
    block0,
    block1,
    aux0,
    aux1,
    terms0,
    terms1,
    away0,
    away1,
    come0,
    come1,
    turned0,
    turned1,
    dq_full0,
    dq_full1,
    dq_away0,
    dq_away1,
    dq_come0,
    dq_come1,
    back,
    row_sem,
    load_sem,
    entered,
    send_sem,
    exchange_recv,
    near_recv,
    two_recv,
    far_recv,
    block_recv,
    up_recv,
    last_recv,
    dq_recv,
    back_recv,
):
    groups, ny, nz, heads, width, half_keys, pieces = sizes
    piece_rows = half_keys // pieces
    counts = (ny, nz)
    held, block, aux = (held0, held1), (block0, block1), (aux0, aux1)
    terms, away, come = (terms0, terms1), (away0, away1), (come0, come1)
    turned = (turned0, turned1)
    dq_full = (dq_full0, dq_full1)
    dq_away, dq_come = (dq_away0, dq_away1), (dq_come0, dq_come1)
    pairs = groups * heads
    scale = 1.0 / math.sqrt(width)

    mine = lax.axis_index("kv")
    place = lax.axis_index("seq")
    y, z = lax.rem(place, ny), lax.div(place, ny)
    position = (y, z)

    def peer(axis, index):
        return (mine, z * ny + index) if axis == 0 else (mine, index * ny + y)

    def around(axis, step):
        return lax.rem(position[axis] + (step % counts[axis]), counts[axis])

    def remote(src, dst, send, recv, device):
        return pltpu.make_async_remote_copy(
            src_ref=src, dst_ref=dst, send_sem=send, recv_sem=recv, device_id=device, device_id_type=MESH
        )

    def wait_bytes(ref, sem):
        remote(ref, ref, send_sem.at[0], sem, (lax.rem(mine + 1, groups), place)).wait_recv()

    row_loads = []
    for index, (source, target) in enumerate(
        ((q_hbm, q_ref), (grad_hbm, grad_ref), (out_hbm, out_ref), (lse_hbm, lse_ref))
    ):
        copy = pltpu.make_async_copy(source, target, row_sem.at[index])
        copy.start()
        row_loads.append(copy)

    barrier = pltpu.get_barrier_semaphore()
    for d in range(1, groups):
        pl.semaphore_signal(barrier, inc=1, device_id=(lax.rem(mine + d, groups), place), device_id_type=MESH)
    for axis in (0, 1):
        for d in near_offsets(counts[axis]):
            pl.semaphore_signal(barrier, inc=1, device_id=peer(axis, around(axis, d)), device_id_type=MESH)

    for half in (0, 1):
        for part, source in ((0, keys_ref), (1, values_ref)):
            pltpu.make_async_copy(
                source.at[pl.ds(half * half_keys, half_keys), :],
                held[half].at[position[half], part],
                load_sem.at[0],
            ).start()

    for copy in row_loads:
        copy.wait()

    def rows_of(ref):
        flat = ref[...].astype(jnp.float32)
        return jnp.concatenate([flat[:, i * width : (i + 1) * width] for i in range(pairs)], axis=0)

    q_rows, grad_rows, out_rows = rows_of(q_ref), rows_of(grad_ref), rows_of(out_ref)
    delta_column = jnp.sum(grad_rows * out_rows, axis=1, keepdims=True)
    eye = lax.broadcasted_iota(jnp.int32, (pairs, pairs), 0) == lax.broadcasted_iota(jnp.int32, (pairs, pairs), 1)
    lse_column = jnp.sum(
        jnp.where(eye, jnp.broadcast_to(lse_ref[...], (pairs, pairs)), 0.0), axis=1, keepdims=True
    )
    lane = lax.broadcasted_iota(jnp.int32, (pairs, LANES), 1)
    member = lax.rem(lax.broadcasted_iota(jnp.int32, (pairs, LANES), 0), heads)
    spot = lane == mine * heads + member
    lse_spots = jnp.where(spot, jnp.broadcast_to(lse_column, (pairs, LANES)), 0.0)
    delta_spots = jnp.where(spot, jnp.broadcast_to(delta_column, (pairs, LANES)), 0.0)
    for group in range(groups):
        rows = slice(group * heads, (group + 1) * heads)
        packet[group] = jnp.concatenate([q_rows[rows], grad_rows[rows]], axis=0).astype(jnp.bfloat16)
        packet_aux[group] = jnp.concatenate(
            [jnp.sum(spots[rows], axis=0, keepdims=True) for spots in (lse_spots, delta_spots)], axis=0
        )

    pl.semaphore_wait(barrier, groups - 1 + len(near_offsets(ny)) + len(near_offsets(nz)))
    relayed = 0
    for axis in (0, 1):
        if counts[axis] > 5:
            relayed += 2
            for d in (2, -2):
                pl.semaphore_signal(entered, inc=1, device_id=peer(axis, around(axis, d)), device_id_type=MESH)

    def exchange(target, origin):
        device = (target, place)
        return (
            remote(packet.at[target], got.at[origin], send_sem.at[0], exchange_recv.at[0], device),
            remote(
                packet_aux.at[target],
                got_aux.at[origin],
                send_sem.at[0],
                exchange_recv.at[1],
                device,
            ),
        )

    for d in other_coords(groups):
        for copy in exchange(lax.rem(mine + d, groups), mine):
            copy.start()
    got[mine] = packet[mine]
    got_aux[mine] = packet_aux[mine]

    every_part = [(kind, piece) for kind in (0, 1) for piece in range(pieces)]
    streams = [(axis, direction) for axis in (0, 1) for direction in (0, 1)]

    def farthest(axis):
        return counts[axis] // 2

    def parts_at(axis, direction, distance):
        kinds = (0, 1) if distance < farthest(axis) else (direction,)
        return [(kind, piece) for kind in kinds for piece in range(pieces)]

    def stop(distance):
        return 2 if distance > 2 else 0

    def toward(direction, steps):
        return steps if direction == 0 else -steps

    def gather_copy(axis, direction, distance, part, arriving=False):
        kind, piece = part
        reach = distance if arriving else stop(distance)
        ref = held[axis].at[around(axis, toward(direction, -reach)), kind, pl.ds(piece * piece_rows, piece_rows), :]
        if distance == 1:
            sem = near_recv.at[axis]
        elif distance == 2:
            sem = two_recv.at[axis, kind * pieces + piece]
        else:
            sem = far_recv.at[axis, distance - 3]
        target = peer(axis, around(axis, toward(direction, distance - stop(distance))))
        return remote(ref, ref, send_sem.at[0], sem, target)

    def gather_wait(axis, distance):
        if distance == 2:
            for direction in (0, 1):
                for part in parts_at(axis, direction, distance):
                    gather_copy(axis, direction, distance, part, True).wait_recv()
        else:
            sem = near_recv.at[axis] if distance == 1 else far_recv.at[axis, distance - 3]
            wait_bytes(held[axis].at[pl.ds(0, 2 if distance < farthest(axis) else 1)], sem)

    loaded = held0.at[pl.ds(0, 2)]
    pltpu.make_async_copy(loaded, loaded, load_sem.at[0]).wait()
    for distance in (2, 1):
        for part in every_part:
            for axis, direction in streams:
                if distance <= farthest(axis) and part in parts_at(axis, direction, distance):
                    gather_copy(axis, direction, distance, part).start()

    wait_bytes(got.at[pl.ds(0, groups - 1)], exchange_recv.at[0])
    wait_bytes(got_aux.at[pl.ds(0, groups - 1)], exchange_recv.at[1])
    if relayed:
        pl.semaphore_wait(entered, relayed)
    got_rows = got[...].astype(jnp.float32)
    own_block = jnp.concatenate(
        [got_rows[i, :heads] for i in range(groups)] + [got_rows[i, heads:] for i in range(groups)], axis=0
    ).astype(jnp.bfloat16)
    got_sum = jnp.sum(got_aux[...], axis=0)
    own_aux = [got_sum[:1], got_sum[1:]]
    per_row = LANES // pairs
    lane_row = lax.broadcasted_iota(jnp.int32, (1, LANES), 1)

    def block_copies(half, target, origin):
        axis = 1 - half
        device = peer(axis, target)
        return (
            remote(
                block[half].at[origin],
                block[half].at[origin],
                send_sem.at[0],
                block_recv.at[half, 0],
                device,
            ),
            remote(
                aux[half].at[origin],
                aux[half].at[origin],
                send_sem.at[0],
                block_recv.at[half, 1],
                device,
            ),
        )

    for half in (0, 1):
        at = position[1 - half]
        block[half][at] = own_block
        inside = lax.div(lane_row, pairs) == lax.rem(at, per_row)
        spread = []
        for vector in own_aux:
            total = vector
            for k in range(1, per_row):
                total = total + pltpu.roll(vector, k * pairs, 1)
            spread.append(jnp.where(inside, total, 0.0))
        aux[half][at] = jnp.concatenate(spread, axis=0)
    for half in (0, 1):
        axis = 1 - half
        for d in reversed(other_coords(counts[axis])):
            for copy in block_copies(half, around(axis, d), position[axis]):
                copy.start()

    for part in every_part:
        for axis, direction in streams:
            if farthest(axis) > 2:
                if direction == 0:
                    kind, piece = part
                    both = held[axis].at[pl.ds(0, 2), kind, pl.ds(piece * piece_rows, piece_rows), :]
                    wait_bytes(both, two_recv.at[axis, kind * pieces + piece])
                for distance in range(3, farthest(axis) + 1):
                    if part in parts_at(axis, direction, distance):
                        gather_copy(axis, direction, distance, part).start()

    lse_rows, delta_rows = [], []
    for half in (0, 1):
        axis = 1 - half
        wait_bytes(block[half].at[pl.ds(0, counts[axis] - 1)], block_recv.at[half, 0])
        wait_bytes(aux[half].at[pl.ds(0, counts[axis] - 1)], block_recv.at[half, 1])
        total_pairs = counts[axis] * pairs
        for index, found in ((0, lse_rows), (1, delta_rows)):
            sums = []
            for first in range(0, counts[axis], per_row):
                piece = aux[half][first, index : index + 1, :]
                for j in range(first + 1, min(first + per_row, counts[axis])):
                    piece = piece + aux[half][j, index : index + 1, :]
                sums.append(piece)
            found.append(jnp.concatenate(sums, axis=1)[:, :total_pairs])
        turned[half][...] = jnp.zeros_like(turned[half])

    def chunks(work):
        across, down = (((1,), (1,)), ((), ())), (((0,), (0,)), ((), ()))
        staged = []
        for half, offsets in work:
            total_pairs = counts[1 - half] * pairs
            q_all = block[half][:, :pairs, :].reshape(total_pairs, width)
            grad_all = block[half][:, pairs:, :].reshape(total_pairs, width)
            places = [around(half, offset) for offset in offsets]
            key = jnp.concatenate([held[half][at, 0] for at in places], axis=0)
            value = jnp.concatenate([held[half][at, 1] for at in places], axis=0)
            scores = lax.dot_general(key, q_all, across, preferred_element_type=jnp.float32)
            dprobs = lax.dot_general(value, grad_all, across, preferred_element_type=jnp.float32)
            staged.append((key, q_all, grad_all, scores, dprobs))
        rounded = []
        for (half, _), (_, _, _, scores, dprobs) in zip(work, staged):
            probs = jnp.exp(scores * scale - lse_rows[half])
            dscores = (probs * (dprobs - delta_rows[half])).astype(jnp.bfloat16)
            rounded.append((probs.astype(jnp.bfloat16), dscores))
        for (half, offsets), (key, q_all, grad_all, _, _), (probs, dscores) in zip(work, staged, rounded):
            dvalue = jnp.dot(probs, grad_all, preferred_element_type=jnp.float32)
            dkey = jnp.dot(dscores, q_all, preferred_element_type=jnp.float32) * scale
            turned[half][...] += lax.dot_general(key, dscores, down, preferred_element_type=jnp.float32)
            for index, offset in enumerate(offsets):
                rows = slice(index * half_keys, (index + 1) * half_keys)
                terms[half][offset % counts[half], 0] = dkey[rows]
                terms[half][offset % counts[half], 1] = dvalue[rows]

    def sum_copy(axis, direction, distance, part):
        kind, piece = part
        rows = pl.ds(piece * piece_rows, piece_rows)
        if distance > 2:
            sem = up_recv.at[axis, direction, kind * pieces + piece]
        else:
            sem = last_recv.at[axis, distance - 1]
        return remote(
            away[axis].at[direction, distance - 1, kind, rows, :],
            come[axis].at[direction, distance - 1, kind, rows, :],
            send_sem.at[0],
            sem,
            peer(axis, around(axis, toward(direction, distance - stop(distance)))),
        )

    def sum_send(distance, axes=(0, 1)):
        for part in every_part:
            kind, piece = part
            rows = pl.ds(piece * piece_rows, piece_rows)
            for axis, direction in streams:
                if axis not in axes or distance > farthest(axis) or part not in parts_at(axis, direction, distance):
                    continue
                total = terms[axis][toward(direction, distance) % counts[axis], kind, rows, :]
                if distance == 2:
                    beyonds = [d for d in range(3, farthest(axis) + 1) if part in parts_at(axis, direction, d)]
                    if beyonds:
                        arrived = come[axis].at[direction, pl.ds(2, len(beyonds)), kind, rows, :]
                        wait_bytes(arrived, up_recv.at[axis, direction, kind * pieces + piece])
                    for beyond in beyonds:
                        total = total + come[axis][direction, beyond - 1, kind, rows, :].astype(jnp.float32)
                away[axis][direction, distance - 1, kind, rows, :] = total.astype(jnp.bfloat16)
                sum_copy(axis, direction, distance, part).start()

    most = max(counts) // 2
    long_axes = [axis for axis in (0, 1) if farthest(axis) > 2]
    for half in long_axes:
        gather_wait(half, 1)
    chunks([(half, (1, -1)) for half in long_axes])
    sum_send(1, long_axes)
    chunks([(half, (0, 2, -2) if farthest(half) > 3 else (0,)) for half in (0, 1)])
    for half in (0, 1):
        gather_wait(half, farthest(half))
    chunks([(half, (farthest(half),)) for half in (0, 1)])
    if most > 2:
        sum_send(most)
    before = [(half, (farthest(half) - 1, 1 - farthest(half))) for half in (0, 1) if farthest(half) > 1]
    for half, offsets in before:
        gather_wait(half, offsets[0])
    chunks(before)
    for distance in range(most - 1, 2, -1):
        sum_send(distance)

    def dq_copy(half, index, group):
        axis = 1 - half
        return remote(
            dq_away[half].at[index, group],
            dq_come[half].at[position[axis], mine],
            send_sem.at[0],
            dq_recv.at[half],
            (group, peer(axis, index)[1]),
        )

    for half in (0, 1):
        axis = 1 - half
        full = jnp.transpose(turned[half][...])
        dq_full[half][...] = full.reshape(counts[axis], pairs, width)
        for index in range(counts[axis]):
            for group in range(groups):
                first = index * pairs + group * heads
                dq_away[half][index, group] = full[first : first + heads].astype(jnp.bfloat16)
        for d in reversed(other_coords(counts[axis])):
            for group in range(groups):
                dq_copy(half, around(axis, d), group).start()

    def back_copy(group):
        return remote(
            back.at[group], dq_come[0].at[position[1], mine], send_sem.at[0], back_recv.at[0], (group, place)
        )

    own_terms = dq_full[0][position[1]] + dq_full[1][position[0]]
    for group in range(groups):
        back[group] = own_terms[group * heads : (group + 1) * heads].astype(jnp.bfloat16)
    for d in other_coords(groups):
        back_copy(lax.rem(mine + d, groups)).start()
    dq_come[0][position[1], mine] = back[mine]

    sum_send(1, [axis for axis in (0, 1) if axis not in long_axes])
    sum_send(2)

    for half in (0, 1):
        axis = 1 - half
        wait_bytes(dq_come[half].at[pl.ds(0, counts[axis] - 1)], dq_recv.at[half])
    wait_bytes(dq_come[0].at[0, pl.ds(0, groups - 1)], back_recv.at[0])
    dq_sum = dq_come[0][position[1]].astype(jnp.float32)
    for half in (0, 1):
        axis = 1 - half
        for d in range(1, counts[axis]):
            dq_sum = dq_sum + dq_come[half][around(axis, d)].astype(jnp.float32)
    dq_ref[...] = (dq_sum * scale).astype(jnp.bfloat16)

    for axis in (0, 1):
        for distance in range(1, min(2, farthest(axis)) + 1):
            whole = come[axis].at[:, distance - 1] if distance < farthest(axis) else come[axis].at[0, distance - 1]
            wait_bytes(whole, last_recv.at[axis, distance - 1])
    for half in (0, 1):
        for kind, result in ((0, dkeys_ref), (1, dvalues_ref)):
            total = terms[half][0, kind]
            for direction in (0, 1):
                for distance in (1, 2):
                    if distance <= farthest(half) and (kind, 0) in parts_at(half, direction, distance):
                        total = total + come[half][direction, distance - 1, kind].astype(jnp.float32)
            result[pl.ds(half * half_keys, half_keys), :] = total.astype(jnp.bfloat16)

    for d in range(1, groups):
        target = lax.rem(mine + d, groups)
        for copy in exchange(target, mine):
            copy.wait_send()
        back_copy(target).wait_send()
    for half in (0, 1):
        axis = 1 - half
        sent = dq_away[half].at[pl.ds(0, counts[axis] - 1)]
        remote(sent, sent, send_sem.at[0], dq_recv.at[half], (lax.rem(mine + 1, groups), place)).wait_send()
        for d in range(1, counts[axis]):
            target = around(axis, d)
            for copy in block_copies(half, target, position[axis]):
                copy.wait_send()
        for direction in (0, 1):
            for distance in range(1, farthest(half) + 1):
                for part in parts_at(half, direction, distance):
                    gather_copy(half, direction, distance, part).wait_send()
                    sum_copy(half, direction, distance, part).wait_send()


def store_kernel(dq_ref, dkeys_ref, dvalues_ref, dq_hbm, dkeys_hbm, dvalues_hbm, dq_row, sem):
    copies = [
        pltpu.make_async_copy(dkeys_ref, dkeys_hbm, sem.at[0]),
        pltpu.make_async_copy(dvalues_ref, dvalues_hbm, sem.at[1]),
        pltpu.make_async_copy(dq_row, dq_hbm, sem.at[2]),
    ]
    copies[0].start()
    copies[1].start()
    groups, heads, width = dq_ref.shape
    for group in range(groups):
        rows = dq_ref[group].astype(jnp.float32)
        for head in range(heads):
            first = (group * heads + head) * width
            dq_row[:, first : first + width] = rows[head : head + 1].astype(jnp.bfloat16)
    copies[2].start()
    for copy in copies:
        copy.wait()


def shards(ny, nz, queries, out_grad, saved_out, saved_lse, video_keys, video_values):
    groups = lax.axis_size("kv")
    width = video_keys.shape[1]
    heads = queries.shape[1] // (groups * width)
    key_rows = video_keys.shape[0]
    half_keys = key_rows // 2
    pairs = groups * heads
    counts = (ny, nz)
    bf16, f32 = jnp.bfloat16, jnp.float32
    dma = pltpu.SemaphoreType.DMA
    across = (counts[1], counts[0])
    pieces = 2
    row = groups * heads * width
    scratch = (
        [pltpu.VMEM((1, row), bf16)] * 3
        + [pltpu.VMEM((1, groups * heads), f32)]
        + [
            pltpu.VMEM((groups, 2 * heads, width), bf16),
            pltpu.VMEM((groups, 2, LANES), f32),
            pltpu.VMEM((groups, 2 * heads, width), bf16),
            pltpu.VMEM((groups, 2, LANES), f32),
        ]
        + [pltpu.VMEM((n, 2, half_keys, width), bf16) for n in counts]
        + [pltpu.VMEM((n, 2 * pairs, width), bf16) for n in across]
        + [pltpu.VMEM((n, 2, LANES), f32) for n in across]
        + [pltpu.VMEM((n, 2, half_keys, width), f32) for n in counts]
        + [pltpu.VMEM((2, n // 2, 2, half_keys, width), bf16) for n in counts]
        + [pltpu.VMEM((2, n // 2, 2, half_keys, width), bf16) for n in counts]
        + [pltpu.VMEM((width, n * pairs), f32) for n in across]
        + [pltpu.VMEM((n, pairs, width), f32) for n in across]
        + [pltpu.VMEM((n, groups, heads, width), bf16) for n in across]
        + [pltpu.VMEM((n, groups, heads, width), bf16) for n in across]
        + [pltpu.VMEM((groups, heads, width), bf16)]
        + [
            dma((4,)),
            dma((1,)),
            pltpu.SemaphoreType.REGULAR,
            dma((1,)),
            dma((2,)),
            dma((2,)),
            dma((2, 2 * pieces)),
            dma((2, 2)),
            dma((2, 2)),
            dma((2, 2, 2 * pieces)),
            dma((2, 2)),
            dma((2,)),
            dma((1,)),
        ]
    )
    vmem = pl.BlockSpec(memory_space=pltpu.VMEM)
    hbm = pl.BlockSpec(memory_space=pltpu.HBM)
    arguments = (queries, out_grad, saved_out, saved_lse, video_keys, video_values)
    arguments = [pltpu.with_memory_space_constraint(argument, pltpu.HBM) for argument in arguments]
    dq, dkeys, dvalues = pl.pallas_call(
        functools.partial(kernel, (groups, ny, nz, heads, width, half_keys, pieces)),
        out_shape=(
            jax.ShapeDtypeStruct((groups, heads, width), bf16),
            jax.ShapeDtypeStruct((key_rows, width), bf16),
            jax.ShapeDtypeStruct((key_rows, width), bf16),
        ),
        in_specs=[hbm] * 6,
        out_specs=(vmem, vmem, vmem),
        scratch_shapes=scratch,
        compiler_params=pltpu.CompilerParams(
            collective_id=0, has_side_effects=True, vmem_limit_bytes=40 * 1024 * 1024
        ),
        name="attention_backward",
    )(*arguments)
    return pl.pallas_call(
        store_kernel,
        out_shape=(
            jax.ShapeDtypeStruct((1, row), bf16),
            jax.ShapeDtypeStruct((key_rows, width), bf16),
            jax.ShapeDtypeStruct((key_rows, width), bf16),
        ),
        in_specs=[vmem] * 3,
        out_specs=(hbm, hbm, hbm),
        scratch_shapes=[pltpu.VMEM((1, row), bf16), dma((3,))],
        compiler_params=pltpu.CompilerParams(vmem_limit_bytes=1024 * 1024),
        name="store_results",
    )(dq, dkeys, dvalues)


def solution(mesh):
    seq = mesh.shape["seq"]
    ny = 1
    while ny * ny < seq:
        ny *= 2
    nz = seq // ny
    rows = P(("kv", "seq"), None)
    keys = P("seq", "kv")
    return jax.shard_map(
        functools.partial(shards, ny, nz),
        mesh=mesh,
        in_specs=(rows, rows, rows, rows, keys, keys),
        out_specs=(rows, keys, keys),
        check_vma=False,
    )
```

```python
import functools
import math

import jax
import jax.numpy as jnp
from jax import lax
from jax.experimental import pallas as pl
from jax.experimental.pallas import tpu as pltpu
from jax.sharding import PartitionSpec as P

MESH = pl.DeviceIdType.MESH
LANES = 128


def other_coords(count):
    return sorted(range(1, count), key=lambda d: (min(d, count - d), d))


def near_offsets(count):
    return [d for d in range(1, count) if min(d, count - d) <= 2]


def kernel(
    sizes,
    q_hbm,
    grad_hbm,
    out_hbm,
    lse_hbm,
    keys_ref,
    values_ref,
    dq_ref,
    dkeys_ref,
    dvalues_ref,
    q_ref,
    grad_ref,
    out_ref,
    lse_ref,
    packet,
    packet_aux,
    got,
    got_aux,
    held0,
    held1,
    block0,
    block1,
    aux0,
    aux1,
    terms0,
    terms1,
    away0,
    away1,
    come0,
    come1,
    turned0,
    turned1,
    dq_full0,
    dq_full1,
    dq_away0,
    dq_away1,
    dq_come0,
    dq_come1,
    back,
    row_sem,
    load_sem,
    entered,
    send_sem,
    exchange_recv,
    near_recv,
    two_recv,
    far_recv,
    block_recv,
    up_recv,
    last_recv,
    dq_recv,
    back_recv,
):
    groups, ny, nz, heads, width, half_keys, pieces = sizes
    piece_rows = half_keys // pieces
    counts = (ny, nz)
    held, block, aux = (held0, held1), (block0, block1), (aux0, aux1)
    terms, away, come = (terms0, terms1), (away0, away1), (come0, come1)
    turned = (turned0, turned1)
    dq_full = (dq_full0, dq_full1)
    dq_away, dq_come = (dq_away0, dq_away1), (dq_come0, dq_come1)
    pairs = groups * heads
    scale = 1.0 / math.sqrt(width)

    mine = lax.axis_index("kv")
    place = lax.axis_index("seq")
    y, z = lax.rem(place, ny), lax.div(place, ny)
    position = (y, z)

    def peer(axis, index):
        return (mine, z * ny + index) if axis == 0 else (mine, index * ny + y)

    def around(axis, step):
        return lax.rem(position[axis] + (step % counts[axis]), counts[axis])

    def remote(src, dst, send, recv, device):
        return pltpu.make_async_remote_copy(
            src_ref=src, dst_ref=dst, send_sem=send, recv_sem=recv, device_id=device, device_id_type=MESH
        )

    def wait_bytes(ref, sem):
        remote(ref, ref, send_sem.at[0], sem, (lax.rem(mine + 1, groups), place)).wait_recv()

    row_loads = []
    for index, (source, target) in enumerate(
        ((q_hbm, q_ref), (grad_hbm, grad_ref), (out_hbm, out_ref), (lse_hbm, lse_ref))
    ):
        copy = pltpu.make_async_copy(source, target, row_sem.at[index])
        copy.start()
        row_loads.append(copy)

    barrier = pltpu.get_barrier_semaphore()
    for d in range(1, groups):
        pl.semaphore_signal(barrier, inc=1, device_id=(lax.rem(mine + d, groups), place), device_id_type=MESH)
    for axis in (0, 1):
        for d in near_offsets(counts[axis]):
            pl.semaphore_signal(barrier, inc=1, device_id=peer(axis, around(axis, d)), device_id_type=MESH)

    for half in (0, 1):
        for part, source in ((0, keys_ref), (1, values_ref)):
            pltpu.make_async_copy(
                source.at[pl.ds(half * half_keys, half_keys), :],
                held[half].at[position[half], part],
                load_sem.at[0],
            ).start()

    for copy in row_loads:
        copy.wait()

    def rows_of(ref):
        flat = ref[...].astype(jnp.float32)
        return jnp.concatenate([flat[:, i * width : (i + 1) * width] for i in range(pairs)], axis=0)

    q_rows, grad_rows, out_rows = rows_of(q_ref), rows_of(grad_ref), rows_of(out_ref)
    delta_column = jnp.sum(grad_rows * out_rows, axis=1, keepdims=True)
    eye = lax.broadcasted_iota(jnp.int32, (pairs, pairs), 0) == lax.broadcasted_iota(jnp.int32, (pairs, pairs), 1)
    lse_column = jnp.sum(
        jnp.where(eye, jnp.broadcast_to(lse_ref[...], (pairs, pairs)), 0.0), axis=1, keepdims=True
    )
    lane = lax.broadcasted_iota(jnp.int32, (pairs, LANES), 1)
    member = lax.rem(lax.broadcasted_iota(jnp.int32, (pairs, LANES), 0), heads)
    spot = lane == mine * heads + member
    lse_spots = jnp.where(spot, jnp.broadcast_to(lse_column, (pairs, LANES)), 0.0)
    delta_spots = jnp.where(spot, jnp.broadcast_to(delta_column, (pairs, LANES)), 0.0)
    for group in range(groups):
        rows = slice(group * heads, (group + 1) * heads)
        packet[group] = jnp.concatenate([q_rows[rows], grad_rows[rows]], axis=0).astype(jnp.bfloat16)
        packet_aux[group] = jnp.concatenate(
            [jnp.sum(spots[rows], axis=0, keepdims=True) for spots in (lse_spots, delta_spots)], axis=0
        )

    pl.semaphore_wait(barrier, groups - 1 + len(near_offsets(ny)) + len(near_offsets(nz)))
    relayed = 0
    for axis in (0, 1):
        if counts[axis] > 5:
            relayed += 2
            for d in (2, -2):
                pl.semaphore_signal(entered, inc=1, device_id=peer(axis, around(axis, d)), device_id_type=MESH)

    def exchange(target, origin):
        device = (target, place)
        return (
            remote(packet.at[target], got.at[origin], send_sem.at[0], exchange_recv.at[0], device),
            remote(
                packet_aux.at[target],
                got_aux.at[origin],
                send_sem.at[0],
                exchange_recv.at[1],
                device,
            ),
        )

    for d in other_coords(groups):
        for copy in exchange(lax.rem(mine + d, groups), mine):
            copy.start()
    got[mine] = packet[mine]
    got_aux[mine] = packet_aux[mine]

    every_part = [(kind, piece) for kind in (0, 1) for piece in range(pieces)]
    streams = [(axis, direction) for axis in (0, 1) for direction in (0, 1)]

    def farthest(axis):
        return counts[axis] // 2

    def parts_at(axis, direction, distance):
        kinds = (0, 1) if distance < farthest(axis) else (direction,)
        return [(kind, piece) for kind in kinds for piece in range(pieces)]

    def stop(distance):
        return 2 if distance > 2 else 0

    def toward(direction, steps):
        return steps if direction == 0 else -steps

    def gather_copy(axis, direction, distance, part, arriving=False):
        kind, piece = part
        reach = distance if arriving else stop(distance)
        ref = held[axis].at[around(axis, toward(direction, -reach)), kind, pl.ds(piece * piece_rows, piece_rows), :]
        if distance == 1:
            sem = near_recv.at[axis]
        elif distance == 2:
            sem = two_recv.at[axis, kind * pieces + piece]
        else:
            sem = far_recv.at[axis, distance - 3]
        target = peer(axis, around(axis, toward(direction, distance - stop(distance))))
        return remote(ref, ref, send_sem.at[0], sem, target)

    def gather_wait(axis, distance):
        if distance == 2:
            for direction in (0, 1):
                for part in parts_at(axis, direction, distance):
                    gather_copy(axis, direction, distance, part, True).wait_recv()
        else:
            sem = near_recv.at[axis] if distance == 1 else far_recv.at[axis, distance - 3]
            wait_bytes(held[axis].at[pl.ds(0, 2 if distance < farthest(axis) else 1)], sem)

    loaded = held0.at[pl.ds(0, 2)]
    pltpu.make_async_copy(loaded, loaded, load_sem.at[0]).wait()
    for distance in (2, 1):
        for part in every_part:
            for axis, direction in streams:
                if distance <= farthest(axis) and part in parts_at(axis, direction, distance):
                    gather_copy(axis, direction, distance, part).start()

    wait_bytes(got.at[pl.ds(0, groups - 1)], exchange_recv.at[0])
    wait_bytes(got_aux.at[pl.ds(0, groups - 1)], exchange_recv.at[1])
    if relayed:
        pl.semaphore_wait(entered, relayed)
    got_rows = got[...].astype(jnp.float32)
    own_block = jnp.concatenate(
        [got_rows[i, :heads] for i in range(groups)] + [got_rows[i, heads:] for i in range(groups)], axis=0
    ).astype(jnp.bfloat16)
    got_sum = jnp.sum(got_aux[...], axis=0)
    own_aux = [got_sum[:1], got_sum[1:]]
    per_row = LANES // pairs
    lane_row = lax.broadcasted_iota(jnp.int32, (1, LANES), 1)

    def block_copies(half, target, origin):
        axis = 1 - half
        device = peer(axis, target)
        return (
            remote(
                block[half].at[origin],
                block[half].at[origin],
                send_sem.at[0],
                block_recv.at[half, 0],
                device,
            ),
            remote(
                aux[half].at[origin],
                aux[half].at[origin],
                send_sem.at[0],
                block_recv.at[half, 1],
                device,
            ),
        )

    for half in (0, 1):
        at = position[1 - half]
        block[half][at] = own_block
        inside = lax.div(lane_row, pairs) == lax.rem(at, per_row)
        spread = []
        for vector in own_aux:
            total = vector
            for k in range(1, per_row):
                total = total + pltpu.roll(vector, k * pairs, 1)
            spread.append(jnp.where(inside, total, 0.0))
        aux[half][at] = jnp.concatenate(spread, axis=0)
    for half in (0, 1):
        axis = 1 - half
        for d in reversed(other_coords(counts[axis])):
            for copy in block_copies(half, around(axis, d), position[axis]):
                copy.start()

    for part in every_part:
        for axis, direction in streams:
            if farthest(axis) > 2:
                if direction == 0:
                    kind, piece = part
                    both = held[axis].at[pl.ds(0, 2), kind, pl.ds(piece * piece_rows, piece_rows), :]
                    wait_bytes(both, two_recv.at[axis, kind * pieces + piece])
                for distance in range(3, farthest(axis) + 1):
                    if part in parts_at(axis, direction, distance):
                        gather_copy(axis, direction, distance, part).start()

    lse_rows, delta_rows = [], []
    for half in (0, 1):
        axis = 1 - half
        wait_bytes(block[half].at[pl.ds(0, counts[axis] - 1)], block_recv.at[half, 0])
        wait_bytes(aux[half].at[pl.ds(0, counts[axis] - 1)], block_recv.at[half, 1])
        total_pairs = counts[axis] * pairs
        for index, found in ((0, lse_rows), (1, delta_rows)):
            sums = []
            for first in range(0, counts[axis], per_row):
                piece = aux[half][first, index : index + 1, :]
                for j in range(first + 1, min(first + per_row, counts[axis])):
                    piece = piece + aux[half][j, index : index + 1, :]
                sums.append(piece)
            found.append(jnp.concatenate(sums, axis=1)[:, :total_pairs])
        turned[half][...] = jnp.zeros_like(turned[half])

    def chunks(work):
        across, down = (((1,), (1,)), ((), ())), (((0,), (0,)), ((), ()))
        staged = []
        for half, offsets in work:
            total_pairs = counts[1 - half] * pairs
            q_all = block[half][:, :pairs, :].reshape(total_pairs, width)
            grad_all = block[half][:, pairs:, :].reshape(total_pairs, width)
            places = [around(half, offset) for offset in offsets]
            key = jnp.concatenate([held[half][at, 0] for at in places], axis=0)
            value = jnp.concatenate([held[half][at, 1] for at in places], axis=0)
            scores = lax.dot_general(key, q_all, across, preferred_element_type=jnp.float32)
            dprobs = lax.dot_general(value, grad_all, across, preferred_element_type=jnp.float32)
            staged.append((key, q_all, grad_all, scores, dprobs))
        rounded = []
        for (half, _), (_, _, _, scores, dprobs) in zip(work, staged):
            probs = jnp.exp(scores * scale - lse_rows[half])
            dscores = (probs * (dprobs - delta_rows[half])).astype(jnp.bfloat16)
            rounded.append((probs.astype(jnp.bfloat16), dscores))
        for (half, offsets), (key, q_all, grad_all, _, _), (probs, dscores) in zip(work, staged, rounded):
            dvalue = jnp.dot(probs, grad_all, preferred_element_type=jnp.float32)
            dkey = jnp.dot(dscores, q_all, preferred_element_type=jnp.float32) * scale
            turned[half][...] += lax.dot_general(key, dscores, down, preferred_element_type=jnp.float32)
            for index, offset in enumerate(offsets):
                rows = slice(index * half_keys, (index + 1) * half_keys)
                terms[half][offset % counts[half], 0] = dkey[rows]
                terms[half][offset % counts[half], 1] = dvalue[rows]

    def sum_copy(axis, direction, distance, part):
        kind, piece = part
        rows = pl.ds(piece * piece_rows, piece_rows)
        if distance > 2:
            sem = up_recv.at[axis, direction, kind * pieces + piece]
        else:
            sem = last_recv.at[axis, distance - 1]
        return remote(
            away[axis].at[direction, distance - 1, kind, rows, :],
            come[axis].at[direction, distance - 1, kind, rows, :],
            send_sem.at[0],
            sem,
            peer(axis, around(axis, toward(direction, distance - stop(distance)))),
        )

    def sum_send(distance, axes=(0, 1)):
        for part in every_part:
            kind, piece = part
            rows = pl.ds(piece * piece_rows, piece_rows)
            for axis, direction in streams:
                if axis not in axes or distance > farthest(axis) or part not in parts_at(axis, direction, distance):
                    continue
                total = terms[axis][toward(direction, distance) % counts[axis], kind, rows, :]
                if distance == 2:
                    beyonds = [d for d in range(3, farthest(axis) + 1) if part in parts_at(axis, direction, d)]
                    if beyonds:
                        arrived = come[axis].at[direction, pl.ds(2, len(beyonds)), kind, rows, :]
                        wait_bytes(arrived, up_recv.at[axis, direction, kind * pieces + piece])
                    for beyond in beyonds:
                        total = total + come[axis][direction, beyond - 1, kind, rows, :].astype(jnp.float32)
                away[axis][direction, distance - 1, kind, rows, :] = total.astype(jnp.bfloat16)
                sum_copy(axis, direction, distance, part).start()

    most = max(counts) // 2
    long_axes = [axis for axis in (0, 1) if farthest(axis) > 2]
    for half in long_axes:
        gather_wait(half, 1)
    chunks([(half, (1, -1)) for half in long_axes])
    sum_send(1, long_axes)
    chunks([(half, (0, 2, -2) if farthest(half) > 3 else (0,)) for half in (0, 1)])
    for half in (0, 1):
        gather_wait(half, farthest(half))
    chunks([(half, (farthest(half),)) for half in (0, 1)])
    if most > 2:
        sum_send(most)
    before = [(half, (farthest(half) - 1, 1 - farthest(half))) for half in (0, 1) if farthest(half) > 1]
    for half, offsets in before:
        gather_wait(half, offsets[0])
    chunks(before)
    for distance in range(most - 1, 2, -1):
        sum_send(distance)

    def dq_copy(half, index, group):
        axis = 1 - half
        return remote(
            dq_away[half].at[index, group],
            dq_come[half].at[position[axis], mine],
            send_sem.at[0],
            dq_recv.at[half],
            (group, peer(axis, index)[1]),
        )

    for half in (0, 1):
        full = jnp.transpose(turned[half][...])
        dq_full[half][...] = full.reshape(counts[1 - half], pairs, width)
    ready = []
    for place_of in range(max(counts) - 1):
        done, ready = ready, []
        for half in (0, 1):
            offsets = other_coords(counts[1 - half])[::-1]
            if place_of < len(offsets):
                index = around(1 - half, offsets[place_of])
                rows = dq_full[half][index]
                for group in range(groups):
                    dq_away[half][index, group] = rows[group * heads : (group + 1) * heads].astype(jnp.bfloat16)
                    ready.append(dq_copy(half, index, group))
        for copy in done:
            copy.start()

    def back_copy(group):
        return remote(
            back.at[group], dq_come[0].at[position[1], mine], send_sem.at[0], back_recv.at[0], (group, place)
        )

    for copy in ready:
        copy.start()
    own_terms = dq_full[0][position[1]] + dq_full[1][position[0]]
    for group in range(groups):
        back[group] = own_terms[group * heads : (group + 1) * heads].astype(jnp.bfloat16)
    for d in other_coords(groups):
        back_copy(lax.rem(mine + d, groups)).start()
    dq_come[0][position[1], mine] = back[mine]

    sum_send(1, [axis for axis in (0, 1) if axis not in long_axes])
    sum_send(2)

    for half in (0, 1):
        axis = 1 - half
        wait_bytes(dq_come[half].at[pl.ds(0, counts[axis] - 1)], dq_recv.at[half])
    wait_bytes(dq_come[0].at[0, pl.ds(0, groups - 1)], back_recv.at[0])
    dq_sum = dq_come[0][position[1]].astype(jnp.float32)
    for half in (0, 1):
        axis = 1 - half
        for d in range(1, counts[axis]):
            dq_sum = dq_sum + dq_come[half][around(axis, d)].astype(jnp.float32)
    dq_ref[...] = (dq_sum * scale).astype(jnp.bfloat16)

    for axis in (0, 1):
        for distance in range(1, min(2, farthest(axis)) + 1):
            whole = come[axis].at[:, distance - 1] if distance < farthest(axis) else come[axis].at[0, distance - 1]
            wait_bytes(whole, last_recv.at[axis, distance - 1])
    for half in (0, 1):
        for kind, result in ((0, dkeys_ref), (1, dvalues_ref)):
            total = terms[half][0, kind]
            for direction in (0, 1):
                for distance in (1, 2):
                    if distance <= farthest(half) and (kind, 0) in parts_at(half, direction, distance):
                        total = total + come[half][direction, distance - 1, kind].astype(jnp.float32)
            result[pl.ds(half * half_keys, half_keys), :] = total.astype(jnp.bfloat16)

    for d in range(1, groups):
        target = lax.rem(mine + d, groups)
        for copy in exchange(target, mine):
            copy.wait_send()
        back_copy(target).wait_send()
    for half in (0, 1):
        axis = 1 - half
        sent = dq_away[half].at[pl.ds(0, counts[axis] - 1)]
        remote(sent, sent, send_sem.at[0], dq_recv.at[half], (lax.rem(mine + 1, groups), place)).wait_send()
        for d in range(1, counts[axis]):
            target = around(axis, d)
            for copy in block_copies(half, target, position[axis]):
                copy.wait_send()
        for direction in (0, 1):
            for distance in range(1, farthest(half) + 1):
                for part in parts_at(half, direction, distance):
                    gather_copy(half, direction, distance, part).wait_send()
                    sum_copy(half, direction, distance, part).wait_send()


def store_kernel(dq_ref, dkeys_ref, dvalues_ref, dq_hbm, dkeys_hbm, dvalues_hbm, dq_row, sem):
    copies = [
        pltpu.make_async_copy(dkeys_ref, dkeys_hbm, sem.at[0]),
        pltpu.make_async_copy(dvalues_ref, dvalues_hbm, sem.at[1]),
        pltpu.make_async_copy(dq_row, dq_hbm, sem.at[2]),
    ]
    copies[0].start()
    copies[1].start()
    groups, heads, width = dq_ref.shape
    for group in range(groups):
        rows = dq_ref[group].astype(jnp.float32)
        for head in range(heads):
            first = (group * heads + head) * width
            dq_row[:, first : first + width] = rows[head : head + 1].astype(jnp.bfloat16)
    copies[2].start()
    for copy in copies:
        copy.wait()


def shards(ny, nz, queries, out_grad, saved_out, saved_lse, video_keys, video_values):
    groups = lax.axis_size("kv")
    width = video_keys.shape[1]
    heads = queries.shape[1] // (groups * width)
    key_rows = video_keys.shape[0]
    half_keys = key_rows // 2
    pairs = groups * heads
    counts = (ny, nz)
    bf16, f32 = jnp.bfloat16, jnp.float32
    dma = pltpu.SemaphoreType.DMA
    across = (counts[1], counts[0])
    pieces = 2
    row = groups * heads * width
    scratch = (
        [pltpu.VMEM((1, row), bf16)] * 3
        + [pltpu.VMEM((1, groups * heads), f32)]
        + [
            pltpu.VMEM((groups, 2 * heads, width), bf16),
            pltpu.VMEM((groups, 2, LANES), f32),
            pltpu.VMEM((groups, 2 * heads, width), bf16),
            pltpu.VMEM((groups, 2, LANES), f32),
        ]
        + [pltpu.VMEM((n, 2, half_keys, width), bf16) for n in counts]
        + [pltpu.VMEM((n, 2 * pairs, width), bf16) for n in across]
        + [pltpu.VMEM((n, 2, LANES), f32) for n in across]
        + [pltpu.VMEM((n, 2, half_keys, width), f32) for n in counts]
        + [pltpu.VMEM((2, n // 2, 2, half_keys, width), bf16) for n in counts]
        + [pltpu.VMEM((2, n // 2, 2, half_keys, width), bf16) for n in counts]
        + [pltpu.VMEM((width, n * pairs), f32) for n in across]
        + [pltpu.VMEM((n, pairs, width), f32) for n in across]
        + [pltpu.VMEM((n, groups, heads, width), bf16) for n in across]
        + [pltpu.VMEM((n, groups, heads, width), bf16) for n in across]
        + [pltpu.VMEM((groups, heads, width), bf16)]
        + [
            dma((4,)),
            dma((1,)),
            pltpu.SemaphoreType.REGULAR,
            dma((1,)),
            dma((2,)),
            dma((2,)),
            dma((2, 2 * pieces)),
            dma((2, 2)),
            dma((2, 2)),
            dma((2, 2, 2 * pieces)),
            dma((2, 2)),
            dma((2,)),
            dma((1,)),
        ]
    )
    vmem = pl.BlockSpec(memory_space=pltpu.VMEM)
    hbm = pl.BlockSpec(memory_space=pltpu.HBM)
    arguments = (queries, out_grad, saved_out, saved_lse, video_keys, video_values)
    arguments = [pltpu.with_memory_space_constraint(argument, pltpu.HBM) for argument in arguments]
    dq, dkeys, dvalues = pl.pallas_call(
        functools.partial(kernel, (groups, ny, nz, heads, width, half_keys, pieces)),
        out_shape=(
            jax.ShapeDtypeStruct((groups, heads, width), bf16),
            jax.ShapeDtypeStruct((key_rows, width), bf16),
            jax.ShapeDtypeStruct((key_rows, width), bf16),
        ),
        in_specs=[hbm] * 6,
        out_specs=(vmem, vmem, vmem),
        scratch_shapes=scratch,
        compiler_params=pltpu.CompilerParams(
            collective_id=0, has_side_effects=True, vmem_limit_bytes=40 * 1024 * 1024
        ),
        name="attention_backward",
    )(*arguments)
    return pl.pallas_call(
        store_kernel,
        out_shape=(
            jax.ShapeDtypeStruct((1, row), bf16),
            jax.ShapeDtypeStruct((key_rows, width), bf16),
            jax.ShapeDtypeStruct((key_rows, width), bf16),
        ),
        in_specs=[vmem] * 3,
        out_specs=(hbm, hbm, hbm),
        scratch_shapes=[pltpu.VMEM((1, row), bf16), dma((3,))],
        compiler_params=pltpu.CompilerParams(vmem_limit_bytes=1024 * 1024),
        name="store_results",
    )(dq, dkeys, dvalues)


def solution(mesh):
    seq = mesh.shape["seq"]
    ny = 1
    while ny * ny < seq:
        ny *= 2
    nz = seq // ny
    rows = P(("kv", "seq"), None)
    keys = P("seq", "kv")
    return jax.shard_map(
        functools.partial(shards, ny, nz),
        mesh=mesh,
        in_specs=(rows, rows, rows, rows, keys, keys),
        out_specs=(rows, keys, keys),
        check_vma=False,
    )
```
